256 devices in a mesh: slab: 32 (over x_hi, z, core), view: 8 (over x_lo, y).
Axes of the slice: x: 4 (x_hi: 2, x_lo: 2; x = x_hi * 2 + x_lo), y: 4, z: 8, core: 2. Of those that a mesh axis runs over, the one named last changes fastest.
Arguments:
- fine_volume: float32 [128, 4096], P('slab'), may hold values from 0 to 1
- coarse_volume: float32 [512, 4096], P('slab'), may hold values from 0 to 1
- fine_rays: bfloat16 [16, 4096, 128], P('view'), may hold values from -0.09375 to 0.09375
- coarse_rays: bfloat16 [16, 4096, 128], P('view'), may hold values from -0.09375 to 0.09375
- fine_axial: bfloat16 [16, 128, 256], P('view', 'slab'), may hold values from -0.3125 to 0.3125
- coarse_axial: bfloat16 [16, 512, 256], P('view', 'slab'), may hold values from -0.21875 to 0.21875
- measured: float32 [256, 16, 128], P('slab', 'view'), may hold values from 0 to 2
- ray_weight: float32 [256, 16, 128], P('slab', 'view'), may hold values from 0.25 to 0.5
- fine_cell_weight: float32 [128, 4096], P('slab'), may hold values from 0.3 to 0.6
- coarse_cell_weight: float32 [512, 4096], P('slab'), may hold values from 0.3 to 0.6
- margin_blocks: int32 [32, 8], P('slab'), may hold values from 0 to 31, as said below
- ray_hits: int32 [16, 32, 8], P('view', 'slab'), may hold values 0 or 1
Outputs:
- fine_result: float32 [128, 4096], P('slab')
- coarse_result: float32 [512, 4096], P('slab')
The draws below stay inside these ranges and needn't reach their ends.
Inputs may be any that keep to these rules, and one draw needn't show every extreme that they name: `margin_blocks`: each row lists 8 different block numbers.
All inputs are finite; a program needn't handle non-finite values. No bound on the sum of `ray_hits` on one device may be relied on, other than what follows from the above.
Results may differ from the reference program's by a relative error of at most 0.005.
Values may be sent and summed in bfloat16 or wider, within the bound.
A program may use at most 64 MiB of HBM per device.

```python
import math
import jax
import jax.numpy as jnp

FXY = 4096
CXY = 4096
DET_U = 128
FZ_DEV = 4
VD = 2
ITERS = 3
TILES = 8
BLOCK = 128
OB = 8
CZ_DEV = 16
FZ = 128
CZ = 512
DET_W = 256
VIEWS = 16
N_SLAB = 32
N_VIEW = 8


def draw_margin_blocks(key, part):
    block_count = CXY // BLOCK
    scores = jax.random.randint(jax.random.fold_in(key, 17), (N_SLAB, block_count), 0, 1 << 20, dtype=jnp.int32)
    scores = scores * block_count + jnp.arange(block_count, dtype=jnp.int32)[None, :]
    order = jnp.argsort(scores, axis=1, stable=True).astype(jnp.int32)
    return order[:, :OB]


def with_ends(entries, key, low, top_value):
    shape = entries.shape
    place = [jax.random.randint(jax.random.fold_in(key, axis), (), 0, shape[axis]) for axis in range(len(shape))]
    entries = entries.at[tuple(place)].set(low)
    longest = shape.index(max(shape))
    place[longest] = (place[longest] + 1) % shape[longest]
    return entries.at[tuple(place)].set(top_value)


def block_scale(rng, dims, cuts, smallest, top_value):
    def one(dim, parts):
        steps = jax.random.uniform(jax.random.fold_in(jax.random.fold_in(rng, 6), dim), (parts,), jnp.float32, smallest / len(cuts), top_value / len(cuts))
        return jnp.repeat(jnp.exp(steps), dims[dim] // parts).reshape((-1,) + (1,) * (len(dims) - dim - 1))

    gain = one(*cuts[0])
    for cut in cuts[1:]:
        gain = gain * one(*cut)
    return gain


def bell_draw(stream_key, dims, spread, limit, split=(), held_as=jnp.bfloat16):
    array = jax.random.normal(stream_key, dims, jnp.float32) * spread
    if len(split) > 0:
        array = block_scale(stream_key, dims, split, -0.22, 0.18) * array
    return jnp.clip(array, min=-limit, max=limit).astype(held_as)


def setup_inputs(seed: int = 0) -> dict:
    key_of = jax.random.split(jax.random.key(seed), 13)
    fine_volume = jnp.clip(1.0 * jax.random.uniform(key_of[0], (FZ, FXY), jnp.float32) ** block_scale(key_of[0], (FZ, FXY), ((0, 32),), -0.2, 0.2), 0.0, 1.0)
    coarse_volume = jnp.clip(1.0 * jax.random.uniform(key_of[1], (CZ, CXY), jnp.float32) ** block_scale(key_of[1], (CZ, CXY), ((0, 32),), -0.2, 0.2), 0.0, 1.0)
    fine_rays = bell_draw(key_of[2], (VIEWS, FXY, DET_U), (FXY + DET_U) ** -0.5, 0.09375, ((0, 8),))
    coarse_rays = bell_draw(key_of[3], (VIEWS, CXY, DET_U), (CXY + DET_U) ** -0.5, 0.09375, ((0, 8),))
    fine_axial = bell_draw(key_of[4], (VIEWS, FZ, DET_W), (FZ + DET_W) ** -0.5, 0.3125, ((0, 8), (1, 32)))
    coarse_axial = bell_draw(key_of[5], (VIEWS, CZ, DET_W), (CZ + DET_W) ** -0.5, 0.21875, ((0, 8), (1, 32)))
    measured = jnp.clip(2.0 * jax.random.uniform(key_of[6], (DET_W, VIEWS, DET_U), jnp.float32) ** block_scale(key_of[6], (DET_W, VIEWS, DET_U), ((0, 32), (1, 8)), -0.2, 0.2), 0.0, 2.0)
    ray_weight = jnp.clip(jnp.exp(math.log(0.5) - 0.6931472 * jax.random.uniform(key_of[7], (DET_W, VIEWS, DET_U), jnp.float32) ** block_scale(key_of[7], (DET_W, VIEWS, DET_U), ((0, 32), (1, 8)), -0.2, 0.2)), 0.25, 0.5)
    fine_cell_weight = jnp.clip(jnp.exp(math.log(0.6) - 0.6931472 * jax.random.uniform(key_of[8], (FZ, FXY), jnp.float32) ** block_scale(key_of[8], (FZ, FXY), ((0, 32),), -0.2, 0.2)), 0.3, 0.6)
    coarse_cell_weight = jnp.clip(jnp.exp(math.log(0.6) - 0.6931472 * jax.random.uniform(key_of[9], (CZ, CXY), jnp.float32) ** block_scale(key_of[9], (CZ, CXY), ((0, 32),), -0.2, 0.2)), 0.3, 0.6)
    margin_blocks = draw_margin_blocks(jax.random.fold_in(key_of[12], 71), 0)
    ray_hits = with_ends((jax.random.randint(key_of[11], (VIEWS, N_SLAB, TILES), 0, 4) < 3).astype(jnp.int32), jax.random.fold_in(key_of[11], 1), 0, 1)
    return {"fine_volume": fine_volume, "coarse_volume": coarse_volume, "fine_rays": fine_rays, "coarse_rays": coarse_rays, "fine_axial": fine_axial, "coarse_axial": coarse_axial, "measured": measured, "ray_weight": ray_weight, "fine_cell_weight": fine_cell_weight, "coarse_cell_weight": coarse_cell_weight, "margin_blocks": margin_blocks, "ray_hits": ray_hits}


def reference(fine_volume, coarse_volume, fine_rays, coarse_rays, fine_axial, coarse_axial, measured, ray_weight, fine_cell_weight, coarse_cell_weight, margin_blocks, ray_hits):
    block_ids = jnp.arange(CXY, dtype=jnp.int32) // BLOCK
    listed = jnp.any(margin_blocks[:, :, None] == block_ids[None, None, :], axis=1)
    keep_mask = jnp.repeat(jnp.where(listed, 0.0, 1.0).astype(jnp.float32), CZ_DEV, axis=0)
    hit_rows = jnp.repeat(ray_hits, DET_W // TILES, axis=2)
    fine_hit = jnp.repeat(hit_rows, FZ_DEV, axis=1).astype(jnp.bfloat16)
    coarse_hit = jnp.repeat(hit_rows, CZ_DEV, axis=1).astype(jnp.bfloat16)
    fine_depth = (fine_axial * fine_hit).astype(jnp.float32)
    coarse_depth = (coarse_axial * coarse_hit).astype(jnp.float32)
    fine_footprint = fine_rays.astype(jnp.float32)
    coarse_footprint = coarse_rays.astype(jnp.float32)
    fine = fine_volume
    coarse = coarse_volume * keep_mask
    for iteration in range(ITERS):
        fine_moment = jnp.einsum('zx,vxu->vzu', fine.astype(jnp.bfloat16).astype(jnp.float32), fine_footprint).astype(jnp.bfloat16).astype(jnp.float32)
        coarse_moment = jnp.einsum('zx,vxu->vzu', coarse.astype(jnp.bfloat16).astype(jnp.float32), coarse_footprint).astype(jnp.bfloat16).astype(jnp.float32)
        projection = jnp.einsum('vzw,vzu->wvu', fine_depth, fine_moment) + jnp.einsum('vzw,vzu->wvu', coarse_depth, coarse_moment)
        residual = (ray_weight * (measured - projection)).astype(jnp.bfloat16).astype(jnp.float32)
        fine_spread = jnp.einsum('vzw,wvu->vzu', fine_depth, residual).astype(jnp.bfloat16).astype(jnp.float32)
        coarse_spread = jnp.einsum('vzw,wvu->vzu', coarse_depth, residual).astype(jnp.bfloat16).astype(jnp.float32)
        fine_group = jnp.einsum('gvzu,gvxu->gzx', fine_spread.reshape(N_VIEW, VD, FZ, DET_U), fine_footprint.reshape(N_VIEW, VD, FXY, DET_U))
        coarse_group = jnp.einsum('gvzu,gvxu->gzx', coarse_spread.reshape(N_VIEW, VD, CZ, DET_U), coarse_footprint.reshape(N_VIEW, VD, CXY, DET_U))
        fine_back = jnp.sum(fine_group.astype(jnp.bfloat16).astype(jnp.float32), axis=0)
        coarse_back = jnp.sum(coarse_group.astype(jnp.bfloat16).astype(jnp.float32), axis=0)
        fine = fine + fine_cell_weight * fine_back
        coarse = (coarse + coarse_cell_weight * coarse_back) * keep_mask
    return fine, coarse
```

```python
import functools

import jax
import jax.numpy as jnp
from jax import lax
from jax.experimental import pallas as pl
from jax.experimental.pallas import tpu as pltpu
from jax.sharding import PartitionSpec as P

ITERS = 3
BLOCK = 128
F32 = jnp.float32
BF16 = jnp.bfloat16


def dot(a, b):
    return lax.dot_general(a, b, (((1,), (0,)), ((), ())), preferred_element_type=F32)


def dot_nt(a, b):
    return lax.dot_general(a, b, (((1,), (1,)), ((), ())), preferred_element_type=F32)


def kernel(
    n_z,
    n_y,
    n_slab,
    n_view,
    fine_volume,
    coarse_volume,
    fine_rays,
    coarse_rays,
    fine_axial,
    coarse_axial,
    measured,
    ray_weight,
    fine_weight,
    coarse_weight,
    margin_blocks,
    ray_hits,
    fine_out,
    coarse_out,
    rays_f,
    rays_c,
    vol_in,
    vol_f,
    wgt_f,
    vol_c,
    wgt_c,
    depth_send,
    depth_all,
    depth_t,
    depth_chip,
    mw_send,
    mw_all,
    moment_send,
    moment_all,
    spread_send,
    spread_recv,
    back_send,
    back_recv,
    sum_send,
    sum_recv,
    load_sem,
    init_send_sem,
    init_recv_sem,
    moment_send_sem,
    moment_recv_sem,
    spread_send_sem,
    spread_recv_sem,
    back_send_sem,
    back_recv_sem,
    sum_send_sem,
    sum_recv_sem,
):
    slab = lax.axis_index("slab")
    view = lax.axis_index("view")
    core = lax.rem(slab, 2)
    z = lax.rem(slab // 2, n_z)
    x_hi = slab // (2 * n_z)
    n_xhi = n_slab // (2 * n_z)
    y = lax.rem(view, n_y)
    x_lo = view // n_y
    n_xlo = n_view // n_y
    partner = slab + 1 - 2 * core
    cells = coarse_volume.shape[1]
    width = cells // n_view
    tiles = width // 128
    rows_f = fine_volume.shape[0]
    rows_w = measured.shape[0]
    all_w = fine_axial.shape[2]
    n_tile = ray_hits.shape[2]

    loads = []
    for i, (src, dst) in enumerate(
        [
            (coarse_volume, vol_c),
            (coarse_weight, wgt_c),
            (fine_volume, vol_in.at[0]),
            (fine_weight, vol_in.at[1]),
        ]
    ):
        copy = pltpu.make_async_copy(src, dst, load_sem.at[i])
        copy.start()
        loads.append(copy)
    ray_loads = []
    for b in range(n_view):
        part = pl.ds(b * width, width)
        pair = []
        for i, (src, dst) in enumerate([(coarse_rays, rays_c), (fine_rays, rays_f)]):
            copy = pltpu.make_async_copy(
                src.at[:, part, :], dst.at[:, part, :], load_sem.at[4 + 2 * b + i]
            )
            copy.start()
            pair.append(copy)
        ray_loads.append(pair)

    barrier = pltpu.get_barrier_semaphore()

    def greet_slab(i, carry):
        other = lax.rem(slab + 1 + i, n_slab)
        pl.semaphore_signal(barrier, inc=1, device_id={"slab": other}, device_id_type=pl.DeviceIdType.MESH)
        return carry

    def greet_view(i, carry):
        other = lax.rem(view + 1 + i, n_view)
        pl.semaphore_signal(barrier, inc=1, device_id={"view": other}, device_id_type=pl.DeviceIdType.MESH)
        return carry

    lax.fori_loop(0, n_slab - 1, greet_slab, 0)
    lax.fori_loop(0, n_view - 1, greet_view, 0)

    row_tile = lax.broadcasted_iota(jnp.int32, (1, all_w), 1) // (all_w // n_tile)
    for v in range(2):
        hit = jnp.zeros((1, all_w), F32)
        for t in range(n_tile):
            hit = jnp.where(row_tile == t, ray_hits[v, 0, t].astype(F32), hit)
        dc = (coarse_axial[v].astype(F32) * hit).astype(BF16)
        df = fine_axial[v].astype(F32) * hit
        df = jnp.concatenate([df, jnp.zeros((8 - rows_f, all_w), F32)], axis=0)
        depth_send[v, 0] = dc[0:8]
        depth_send[v, 1] = dc[8:16]
        depth_send[v, 2] = df.astype(BF16)
        mw_send[v, 0] = measured[:, v, :]
        mw_send[v, 1] = ray_weight[:, v, :]
    depth_all[slab] = depth_send[core]
    mw_all[slab] = mw_send[core]

    for copy in loads:
        copy.wait()
    block_id = lax.broadcasted_iota(jnp.int32, (1, cells), 1) // BLOCK
    keep = jnp.ones((1, cells), F32)
    for t in range(margin_blocks.shape[1]):
        keep = jnp.where(block_id == margin_blocks[0, t], 0.0, keep)
    vol_c[...] = vol_c[...] * keep
    wgt_c[...] = wgt_c[...] * keep
    for b in range(n_view):
        for j in range(tiles):
            part = slice(b * width + j * 128, b * width + (j + 1) * 128)
            vol_f[b, j * rows_f : (j + 1) * rows_f, :] = vol_in[0, :, part]
            wgt_f[b, j * rows_f : (j + 1) * rows_f, :] = vol_in[1, :, part]

    group = lax.broadcasted_iota(jnp.int32, (16, 128), 0) // rows_f
    masks = [jnp.where(group == j, 1.0, 0.0).astype(F32) for j in range(tiles)]

    def add_moment(b, acc):
        part = pl.ds(pl.multiple_of(b * width, 128), width)
        lhs_c = vol_c[:, part].astype(BF16)
        packed = vol_f[b]
        lhs_f = jnp.concatenate([(packed * m).astype(BF16) for m in masks], axis=1)
        new = []
        for v in range(2):
            new.append(acc[v] + dot(lhs_c, rays_c[v, part, :]))
        for v in range(2):
            new.append(acc[2 + v] + dot(lhs_f, rays_f[v, part, :]))
        return new

    def finish_moment(k, acc):
        for v in range(2):
            mc = acc[v].astype(BF16)
            half = acc[2 + v][0:8] + acc[2 + v][8:16]
            whole = half + pltpu.roll(half, 4, 0)
            moment_send[k, v, 0] = mc[0:8]
            moment_send[k, v, 1] = mc[8:16]
            moment_send[k, v, 2] = whole.astype(BF16)
        moment_all[k, slab] = moment_send[k, core]

    zero = [jnp.zeros((16, 128), F32) for _ in range(4)]
    acc = zero
    for b in range(n_view):
        for copy in ray_loads[b]:
            copy.wait()
        acc = add_moment(b, acc)
    finish_moment(0, acc)

    pl.semaphore_wait(barrier, n_slab + n_view - 2)

    def to_slab(src, dst, send_sem, recv_sem, other):
        return pltpu.make_async_remote_copy(
            src_ref=src,
            dst_ref=dst,
            send_sem=send_sem,
            recv_sem=recv_sem,
            device_id={"slab": other},
            device_id_type=pl.DeviceIdType.MESH,
        )

    n_chip = n_xhi * n_z

    def each_slab(send):
        def step(i, carry):
            turn = lax.rem(i, n_z)
            half = (turn + 1) // 2
            dz = n_z // 2 + half * (2 * lax.rem(turn, 2) - 1)
            dx = n_xhi - 1 - i // n_z
            chip = lax.rem(x_hi + dx, n_xhi) * n_z + lax.rem(z + dz + n_z, n_z)
            for c in range(2):
                send(2 * chip + c, c)
            return carry

        lax.fori_loop(0, n_chip - 1, step, 0)
        send(partner, 1 - core)

    def send_init(other, c):
        to_slab(
            depth_send.at[c], depth_all.at[slab], init_send_sem.at[0], init_recv_sem.at[0], other
        ).start()
        to_slab(
            mw_send.at[c], mw_all.at[slab], init_send_sem.at[1], init_recv_sem.at[1], other
        ).start()

    def send_moments(k):
        def send(other, c):
            to_slab(
                moment_send.at[k, c],
                moment_all.at[k, slab],
                moment_send_sem.at[k],
                moment_recv_sem.at[k],
                other,
            ).start()

        each_slab(send)

    def others(ref, sem_send, sem_recv, count):
        return pltpu.make_async_remote_copy(
            src_ref=ref.at[pl.ds(0, count)],
            dst_ref=ref.at[pl.ds(0, count)],
            send_sem=sem_send,
            recv_sem=sem_recv,
            device_id={"slab": partner},
            device_id_type=pl.DeviceIdType.MESH,
        )

    each_slab(send_init)
    send_moments(0)

    others(depth_all, init_send_sem.at[0], init_recv_sem.at[0], n_slab - 1).wait_recv()
    depth_t[...] = depth_all[...].reshape(n_slab * 24, all_w).T
    depth_chip[0] = depth_all[slab].reshape(24, all_w)
    depth_chip[1] = depth_all[partner].reshape(24, all_w)
    others(mw_all, init_send_sem.at[1], init_recv_sem.at[1], n_slab - 1).wait_recv()

    view_order = sorted(
        [(dx, dy) for dx in range(n_xlo) for dy in range(n_y)],
        key=lambda p: -(p[0] + min(p[1], n_y - p[1])),
    )

    def view_of(step):
        dx, dy = step
        return lax.rem(x_lo + dx, n_xlo) * n_y + lax.rem(y + dy, n_y)

    def to_view(src, dst, send_sem, recv_sem, other):
        return pltpu.make_async_remote_copy(
            src_ref=src,
            dst_ref=dst,
            send_sem=send_sem,
            recv_sem=recv_sem,
            device_id={"view": other},
            device_id_type=pl.DeviceIdType.MESH,
        )

    for k in range(ITERS):
        if k > 0:
            send_moments(k)
        others(moment_all.at[k], moment_send_sem.at[k], moment_recv_sem.at[k], n_slab - 1).wait_recv()
        moments = moment_all[k].reshape(n_slab * 24, 128)
        projection = dot(depth_t[...], moments)
        seen = mw_all[:, 0].reshape(n_slab * rows_w, 128)
        weight = mw_all[:, 1].reshape(n_slab * rows_w, 128)
        residual = (weight * (seen - projection)).astype(BF16)
        spread_other = dot(depth_chip[1], residual).astype(BF16)
        for i in range(3):
            spread_send[k, i] = spread_other[8 * i : 8 * (i + 1)]
        hand = to_slab(
            spread_send.at[k], spread_recv.at[k], spread_send_sem.at[k], spread_recv_sem.at[k], partner
        )
        hand.start()
        spread_own = dot(depth_chip[0], residual)
        hand.wait_recv()

        def operands(spread):
            coarse = spread[0:16].astype(BF16)
            fine = spread[16:24].astype(BF16).astype(F32)
            fine = fine + pltpu.roll(fine, 4, 0)
            fine = jnp.concatenate([fine, fine], axis=0)
            return coarse, [(fine * m).astype(BF16) for m in masks]

        own_c, own_f = operands(spread_own)
        other_c, other_f = operands(spread_recv[k].astype(F32).reshape(24, 128))
        for step in view_order:
            b = view_of(step)
            base = b * width
            part = pl.ds(pl.multiple_of(base, 128), width)
            term_c = dot_nt(own_c, rays_c[core, part, :]) + dot_nt(other_c, rays_c[1 - core, part, :])
            term_f = jnp.zeros((16, 128), F32)
            for j in range(tiles):
                piece = pl.ds(pl.multiple_of(base + j * 128, 128), 128)
                term_f = term_f + dot_nt(own_f[j], rays_f[core, piece, :])
                term_f = term_f + dot_nt(other_f[j], rays_f[1 - core, piece, :])
            dest = back_recv.at[k, view] if step == (0, 0) else back_send.at[k, b]
            for j in range(tiles):
                dest[j] = term_c[:, j * 128 : (j + 1) * 128].astype(BF16)
            dest[tiles] = term_f.astype(BF16)
            if step != (0, 0):
                to_view(
                    back_send.at[k, b],
                    back_recv.at[k, view],
                    back_send_sem.at[k],
                    back_recv_sem.at[k, view],
                    b,
                ).start()
        total = back_recv[k, view].astype(F32)
        for step in reversed(view_order):
            if step == (0, 0):
                continue
            b = view_of(step)
            to_view(
                back_send.at[k, b], back_recv.at[k, b], back_send_sem.at[k], back_recv_sem.at[k, b], b
            ).wait_recv()
            total = total + back_recv[k, b].astype(F32)
        sum_send[k] = total.astype(BF16)
        for step in view_order:
            if step == (0, 0):
                continue
            to_view(
                sum_send.at[k],
                sum_recv.at[k, view],
                sum_send_sem.at[k],
                sum_recv_sem.at[k, view],
                view_of(step),
            ).start()
        acc = zero
        for step in reversed(view_order):
            b = view_of(step)
            if step == (0, 0):
                back = sum_send[k].astype(F32)
            else:
                to_view(
                    sum_send.at[k], sum_recv.at[k, b], sum_send_sem.at[k], sum_recv_sem.at[k, b], b
                ).wait_recv()
                back = sum_recv[k, b].astype(F32)
            for j in range(tiles):
                piece = pl.ds(pl.multiple_of(b * width + j * 128, 128), 128)
                vol_c[:, piece] = vol_c[:, piece] + wgt_c[:, piece] * back[j]
            vol_f[b] = vol_f[b] + wgt_f[b] * back[tiles]
            if k < ITERS - 1:
                acc = add_moment(b, acc)
        if k < ITERS - 1:
            finish_moment(k + 1, acc)

    coarse_out[...] = vol_c[...]
    for b in range(n_view):
        for j in range(tiles):
            part = slice(b * width + j * 128, b * width + (j + 1) * 128)
            fine_out[:, part] = vol_f[b, j * rows_f : (j + 1) * rows_f, :]

    others(depth_all, init_send_sem.at[0], init_recv_sem.at[0], n_slab - 1).wait_send()
    others(mw_all, init_send_sem.at[1], init_recv_sem.at[1], n_slab - 1).wait_send()
    for k in range(ITERS):
        others(
            moment_all.at[k], moment_send_sem.at[k], moment_recv_sem.at[k], n_slab - 1
        ).wait_send()
        to_slab(
            spread_send.at[k], spread_recv.at[k], spread_send_sem.at[k], spread_recv_sem.at[k], partner
        ).wait_send()
        others(back_send.at[k], back_send_sem.at[k], back_recv_sem.at[k, 0], n_view - 1).wait_send()
        others(back_send.at[k], sum_send_sem.at[k], back_recv_sem.at[k, 0], n_view - 1).wait_send()


def build(mesh, n_z, n_y):
    n_slab, n_view = mesh.shape["slab"], mesh.shape["view"]

    def body(*args):
        fine_volume, coarse_volume = args[0], args[1]
        rows_f, cells = fine_volume.shape
        rows_c = coarse_volume.shape[0]
        all_w = args[4].shape[2]
        rows_w = args[6].shape[0]
        width = cells // n_view
        tiles = width // 128
        anyspace = pl.BlockSpec(memory_space=pl.ANY)
        vmem = pl.BlockSpec(memory_space=pltpu.VMEM)
        smem = pl.BlockSpec(memory_space=pltpu.SMEM)
        dma = pltpu.SemaphoreType.DMA
        block = (tiles + 1, 16, 128)
        return pl.pallas_call(
            functools.partial(kernel, n_z, n_y, n_slab, n_view),
            name="sirt",
            out_shape=(
                jax.ShapeDtypeStruct((rows_f, cells), F32),
                jax.ShapeDtypeStruct((rows_c, cells), F32),
            ),
            in_specs=[anyspace] * 4 + [vmem] * 4 + [anyspace] * 2 + [smem] * 2,
            out_specs=(vmem, vmem),
            scratch_shapes=[
                pltpu.VMEM((2, cells, 128), BF16),
                pltpu.VMEM((2, cells, 128), BF16),
                pltpu.VMEM((2, rows_f, cells), F32),
                pltpu.VMEM((n_view, 16, 128), F32),
                pltpu.VMEM((n_view, 16, 128), F32),
                pltpu.VMEM((rows_c, cells), F32),
                pltpu.VMEM((rows_c, cells), F32),
                pltpu.VMEM((2, 3, 8, all_w), BF16),
                pltpu.VMEM((n_slab, 3, 8, all_w), BF16),
                pltpu.VMEM((all_w, n_slab * 24), BF16),
                pltpu.VMEM((2, 24, all_w), BF16),
                pltpu.VMEM((2, 2, rows_w, 128), F32),
                pltpu.VMEM((n_slab, 2, rows_w, 128), F32),
                pltpu.VMEM((ITERS, 2, 3, 8, 128), BF16),
                pltpu.VMEM((ITERS, n_slab, 3, 8, 128), BF16),
                pltpu.VMEM((ITERS, 3, 8, 128), BF16),
                pltpu.VMEM((ITERS, 3, 8, 128), BF16),
                pltpu.VMEM((ITERS, n_view) + block, BF16),
                pltpu.VMEM((ITERS, n_view) + block, BF16),
                pltpu.VMEM((ITERS,) + block, BF16),
                pltpu.VMEM((ITERS, n_view) + block, BF16),
                dma((4 + 2 * n_view,)),
                dma((2,)),
                dma((2,)),
                dma((ITERS,)),
                dma((ITERS,)),
                dma((ITERS,)),
                dma((ITERS,)),
                dma((ITERS,)),
                dma((ITERS, n_view)),
                dma((ITERS,)),
                dma((ITERS, n_view)),
            ],
            compiler_params=pltpu.CompilerParams(collective_id=0, has_side_effects=True),
        )(*args)

    return jax.shard_map(
        body,
        mesh=mesh,
        in_specs=(
            P("slab", None),
            P("slab", None),
            P("view", None, None),
            P("view", None, None),
            P("view", "slab", None),
            P("view", "slab", None),
            P("slab", "view", None),
            P("slab", "view", None),
            P("slab", None),
            P("slab", None),
            P("slab", None),
            P("view", "slab", None),
        ),
        out_specs=(P("slab", None), P("slab", None)),
        check_vma=False,
    )


def solution(mesh):
    return build(mesh, 8, 4)
```

```python
import functools

import jax
import jax.numpy as jnp
from jax import lax
from jax.experimental import pallas as pl
from jax.experimental.pallas import tpu as pltpu
from jax.sharding import PartitionSpec as P

ITERS = 3
BLOCK = 128
F32 = jnp.float32
BF16 = jnp.bfloat16


def dot(a, b):
    return lax.dot_general(a, b, (((1,), (0,)), ((), ())), preferred_element_type=F32)


def dot_nt(a, b):
    return lax.dot_general(a, b, (((1,), (1,)), ((), ())), preferred_element_type=F32)


def kernel(
    n_z,
    n_y,
    n_slab,
    n_view,
    fine_volume,
    coarse_volume,
    fine_rays,
    coarse_rays,
    fine_axial,
    coarse_axial,
    measured,
    ray_weight,
    fine_weight,
    coarse_weight,
    margin_blocks,
    ray_hits,
    fine_out,
    coarse_out,
    rays_f,
    rays_c,
    axial_f,
    axial_c,
    seen_in,
    weight_in,
    blocks,
    hits,
    vol_in,
    vol_f,
    wgt_f,
    vol_c,
    wgt_c,
    init_send,
    init_all,
    depth_t,
    depth_chip,
    seen,
    weight,
    moment_send,
    moment_all,
    spread_send,
    spread_recv,
    back_own,
    back_send,
    back_recv,
    sum_send,
    sum_recv,
    load_sem,
    init_send_sem,
    init_recv_sem,
    moment_send_sem,
    moment_recv_sem,
    spread_send_sem,
    spread_recv_sem,
    back_send_sem,
    back_recv_sem,
    sum_send_sem,
    sum_recv_sem,
):
    slab = lax.axis_index("slab")
    view = lax.axis_index("view")
    core = lax.rem(slab, 2)
    z = lax.rem(slab // 2, n_z)
    x_hi = slab // (2 * n_z)
    n_xhi = n_slab // (2 * n_z)
    y = lax.rem(view, n_y)
    x_lo = view // n_y
    n_xlo = n_view // n_y
    partner = slab + 1 - 2 * core
    cells = coarse_volume.shape[1]
    width = cells // n_view
    tiles = width // 128
    rows_f = fine_volume.shape[0]
    rows_w = measured.shape[0]
    all_w = fine_axial.shape[2]
    n_tile = ray_hits.shape[2]

    barrier = pltpu.get_barrier_semaphore()

    def greet_slab(i, carry):
        other = lax.rem(slab + 1 + i, n_slab)
        pl.semaphore_signal(barrier, inc=1, device_id={"slab": other}, device_id_type=pl.DeviceIdType.MESH)
        return carry

    def greet_view(i, carry):
        other = lax.rem(view + 1 + i, n_view)
        pl.semaphore_signal(barrier, inc=1, device_id={"view": other}, device_id_type=pl.DeviceIdType.MESH)
        return carry

    lax.fori_loop(0, n_slab - 1, greet_slab, 0)
    lax.fori_loop(0, n_view - 1, greet_view, 0)

    loads = []
    for i, (src, dst) in enumerate(
        [
            (ray_hits, hits),
            (fine_axial, axial_f),
            (coarse_axial, axial_c),
            (measured, seen_in),
            (ray_weight, weight_in),
            (margin_blocks, blocks),
            (coarse_volume, vol_c),
            (coarse_weight, wgt_c),
            (fine_volume, vol_in.at[0]),
            (fine_weight, vol_in.at[1]),
        ]
    ):
        copy = pltpu.make_async_copy(src, dst, load_sem.at[i])
        copy.start()
        loads.append(copy)
    ray_loads = []
    for b in range(n_view):
        part = pl.ds(b * width, width)
        pair = []
        for i, (src, dst) in enumerate([(coarse_rays, rays_c), (fine_rays, rays_f)]):
            copy = pltpu.make_async_copy(
                src.at[:, part, :], dst.at[:, part, :], load_sem.at[10 + 2 * b + i]
            )
            copy.start()
            pair.append(copy)
        ray_loads.append(pair)

    for copy in loads[:5]:
        copy.wait()
    half_w = all_w // 2
    row_tile = lax.broadcasted_iota(jnp.int32, (1, all_w), 1) // (all_w // n_tile)
    for v in range(2):
        hit = jnp.zeros((1, all_w), F32)
        for t in range(n_tile):
            hit = jnp.where(row_tile == t, hits[v, 0, t].astype(F32), hit)
        dc = (axial_c[v].astype(F32) * hit).astype(BF16)
        df = axial_f[v].astype(F32) * hit
        df = jnp.concatenate([df[:, :half_w], df[:, half_w:]], axis=0)
        init_send[v, 0] = dc[0:8, :half_w]
        init_send[v, 1] = dc[8:16, :half_w]
        init_send[v, 2] = dc[0:8, half_w:]
        init_send[v, 3] = dc[8:16, half_w:]
        init_send[v, 4] = df.astype(BF16)
        init_send[v, 5] = seen_in[:, v, :].astype(BF16)
        init_send[v, 6] = weight_in[:, v, :].astype(BF16)
    init_all[slab] = init_send[core]

    for copy in loads[5:]:
        copy.wait()
    block_id = lax.broadcasted_iota(jnp.int32, (1, cells), 1) // BLOCK
    keep = jnp.ones((1, cells), F32)
    for t in range(margin_blocks.shape[1]):
        keep = jnp.where(block_id == blocks[0, t], 0.0, keep)
    vol_c[...] = vol_c[...] * keep
    wgt_c[...] = wgt_c[...] * keep
    for b in range(n_view):
        for j in range(tiles):
            part = slice(b * width + j * 128, b * width + (j + 1) * 128)
            vol_f[b, j * rows_f : (j + 1) * rows_f, :] = vol_in[0, :, part]
            wgt_f[b, j * rows_f : (j + 1) * rows_f, :] = vol_in[1, :, part]

    group = lax.broadcasted_iota(jnp.int32, (16, 128), 0) // rows_f
    masks = [jnp.where(group == j, 1.0, 0.0).astype(F32) for j in range(tiles)]

    def add_moment(b, acc):
        part = pl.ds(pl.multiple_of(b * width, 128), width)
        lhs_c = vol_c[:, part].astype(BF16)
        packed = vol_f[b]
        lhs_f = jnp.concatenate([(packed * m).astype(BF16) for m in masks], axis=1)
        new = []
        for v in range(2):
            new.append(acc[v] + dot(lhs_c, rays_c[v, part, :]))
        for v in range(2):
            new.append(acc[2 + v] + dot(lhs_f, rays_f[v, part, :]))
        return new

    def finish_moment(k, acc):
        for v in range(2):
            mc = acc[v].astype(BF16)
            half = acc[2 + v][0:8] + acc[2 + v][8:16]
            whole = half + pltpu.roll(half, 4, 0)
            moment_send[k, v, 0] = mc[0:8]
            moment_send[k, v, 1] = mc[8:16]
            moment_send[k, v, 2] = whole.astype(BF16)
        moment_all[k, slab] = moment_send[k, core]

    zero = [jnp.zeros((16, 128), F32) for _ in range(4)]
    acc = zero
    for b in range(n_view):
        for copy in ray_loads[b]:
            copy.wait()
        acc = add_moment(b, acc)
    finish_moment(0, acc)

    pl.semaphore_wait(barrier, n_slab + n_view - 2)

    def to_slab(src, dst, send_sem, recv_sem, other):
        return pltpu.make_async_remote_copy(
            src_ref=src,
            dst_ref=dst,
            send_sem=send_sem,
            recv_sem=recv_sem,
            device_id={"slab": other},
            device_id_type=pl.DeviceIdType.MESH,
        )

    n_chip = n_xhi * n_z

    def each_slab(send):
        def step(i, carry):
            turn = lax.rem(i, n_z)
            half = (turn + 1) // 2
            dz = n_z // 2 + half * (2 * lax.rem(turn, 2) - 1)
            dx = n_xhi - 1 - i // n_z
            chip = lax.rem(x_hi + dx, n_xhi) * n_z + lax.rem(z + dz + n_z, n_z)
            for c in range(2):
                send(2 * chip + c, c)
            return carry

        lax.fori_loop(0, n_chip - 1, step, 0)
        send(partner, 1 - core)

    def send_init(other, c):
        to_slab(
            init_send.at[c], init_all.at[slab], init_send_sem.at[0], init_recv_sem.at[0], other
        ).start()

    def send_moments(k):
        def send(other, c):
            to_slab(
                moment_send.at[k, c],
                moment_all.at[k, slab],
                moment_send_sem.at[k],
                moment_recv_sem.at[k],
                other,
            ).start()

        each_slab(send)

    def others(ref, sem_send, sem_recv, count):
        return pltpu.make_async_remote_copy(
            src_ref=ref.at[pl.ds(0, count)],
            dst_ref=ref.at[pl.ds(0, count)],
            send_sem=sem_send,
            recv_sem=sem_recv,
            device_id={"slab": partner},
            device_id_type=pl.DeviceIdType.MESH,
        )

    each_slab(send_init)
    send_moments(0)

    others(init_all, init_send_sem.at[0], init_recv_sem.at[0], n_slab - 1).wait_recv()
    upper = lax.broadcasted_iota(jnp.int32, (8, 128), 0) >= rows_f
    for h in range(2):
        cols = slice(h * half_w, (h + 1) * half_w)
        fine = init_all[:, 4].astype(F32)
        fine = jnp.where(upper if h else jnp.logical_not(upper), fine, 0.0).astype(BF16)
        depth = jnp.concatenate(
            [init_all[:, 2 * h], init_all[:, 2 * h + 1], fine], axis=1
        ).reshape(n_slab * 24, half_w)
        depth_t[cols, :] = depth.T
        for i, index in enumerate((slab, partner)):
            own = init_all[index, 4].astype(F32)
            own = jnp.where(upper if h else jnp.logical_not(upper), own, 0.0).astype(BF16)
            depth_chip[i, 0:8, cols] = init_all[index, 2 * h]
            depth_chip[i, 8:16, cols] = init_all[index, 2 * h + 1]
            depth_chip[i, 16:24, cols] = own
    seen[...] = init_all[:, 5].astype(F32).reshape(n_slab * rows_w, 128)
    weight[...] = init_all[:, 6].astype(F32).reshape(n_slab * rows_w, 128)

    view_order = sorted(
        [(dx, dy) for dx in range(n_xlo) for dy in range(n_y)],
        key=lambda p: -(p[0] + min(p[1], n_y - p[1])),
    )

    def view_of(step):
        dx, dy = step
        return lax.rem(x_lo + dx, n_xlo) * n_y + lax.rem(y + dy, n_y)

    def to_view(src, dst, send_sem, recv_sem, other):
        return pltpu.make_async_remote_copy(
            src_ref=src,
            dst_ref=dst,
            send_sem=send_sem,
            recv_sem=recv_sem,
            device_id={"view": other},
            device_id_type=pl.DeviceIdType.MESH,
        )

    for k in range(ITERS):
        if k > 0:
            send_moments(k)
        others(moment_all.at[k], moment_send_sem.at[k], moment_recv_sem.at[k], n_slab - 1).wait_recv()
        moments = moment_all[k].reshape(n_slab * 24, 128)
        projection = dot(depth_t[...], moments)
        residual = (weight[...] * (seen[...] - projection)).astype(BF16)

        def spread_of(depth):
            spread = dot(depth, residual)
            fine = spread[16:24]
            return jnp.concatenate([spread[0:16], fine + pltpu.roll(fine, 4, 0)], axis=0).astype(BF16)

        spread_other = spread_of(depth_chip[1])
        for i in range(3):
            spread_send[k, i] = spread_other[8 * i : 8 * (i + 1)]
        hand = to_slab(
            spread_send.at[k], spread_recv.at[k], spread_send_sem.at[k], spread_recv_sem.at[k], partner
        )
        hand.start()
        spread_own = spread_of(depth_chip[0])

        def operands(spread):
            fine = spread[16:24].astype(F32)
            fine = jnp.concatenate([fine, fine], axis=0)
            return spread[0:16], [(fine * m).astype(BF16) for m in masks]

        def terms(coarse, fine, v, b):
            base = b * width
            part = pl.ds(pl.multiple_of(base, 128), width)
            term_c = dot_nt(coarse, rays_c[v, part, :])
            term_f = jnp.zeros((16, 128), F32)
            for j in range(tiles):
                piece = pl.ds(pl.multiple_of(base + j * 128, 128), 128)
                term_f = term_f + dot_nt(fine[j], rays_f[v, piece, :])
            return term_c, term_f

        own_c, own_f = operands(spread_own)
        for i, step in enumerate(view_order):
            term_c, term_f = terms(own_c, own_f, core, view_of(step))
            back_own[i, :, 0:width] = term_c
            back_own[i, :, width : width + 128] = term_f
        hand.wait_recv()
        other_c, other_f = operands(spread_recv[k].reshape(24, 128))
        for i, step in enumerate(view_order):
            b = view_of(step)
            term_c, term_f = terms(other_c, other_f, 1 - core, b)
            term_c = term_c + back_own[i, :, 0:width]
            term_f = term_f + back_own[i, :, width : width + 128]
            dest = back_recv.at[k, view] if step == (0, 0) else back_send.at[k, b]
            for j in range(tiles):
                dest[j] = term_c[:, j * 128 : (j + 1) * 128].astype(BF16)
            dest[tiles] = term_f.astype(BF16)
            if step != (0, 0):
                to_view(
                    back_send.at[k, b],
                    back_recv.at[k, view],
                    back_send_sem.at[k],
                    back_recv_sem.at[k, view],
                    b,
                ).start()
        total = back_recv[k, view].astype(F32)
        for step in reversed(view_order):
            if step == (0, 0):
                continue
            b = view_of(step)
            to_view(
                back_send.at[k, b], back_recv.at[k, b], back_send_sem.at[k], back_recv_sem.at[k, b], b
            ).wait_recv()
            total = total + back_recv[k, b].astype(F32)
        sum_send[k] = total.astype(BF16)
        for step in view_order:
            if step == (0, 0):
                continue
            to_view(
                sum_send.at[k],
                sum_recv.at[k, view],
                sum_send_sem.at[k],
                sum_recv_sem.at[k, view],
                view_of(step),
            ).start()
        acc = zero
        for step in reversed(view_order):
            b = view_of(step)
            if step == (0, 0):
                back = sum_send[k].astype(F32)
            else:
                to_view(
                    sum_send.at[k], sum_recv.at[k, b], sum_send_sem.at[k], sum_recv_sem.at[k, b], b
                ).wait_recv()
                back = sum_recv[k, b].astype(F32)
            for j in range(tiles):
                piece = pl.ds(pl.multiple_of(b * width + j * 128, 128), 128)
                vol_c[:, piece] = vol_c[:, piece] + wgt_c[:, piece] * back[j]
            vol_f[b] = vol_f[b] + wgt_f[b] * back[tiles]
            if k < ITERS - 1:
                acc = add_moment(b, acc)
        if k < ITERS - 1:
            finish_moment(k + 1, acc)

    coarse_out[...] = vol_c[...]
    for b in range(n_view):
        for j in range(tiles):
            part = slice(b * width + j * 128, b * width + (j + 1) * 128)
            fine_out[:, part] = vol_f[b, j * rows_f : (j + 1) * rows_f, :]

    others(init_all, init_send_sem.at[0], init_recv_sem.at[0], n_slab - 1).wait_send()
    for k in range(ITERS):
        others(
            moment_all.at[k], moment_send_sem.at[k], moment_recv_sem.at[k], n_slab - 1
        ).wait_send()
        to_slab(
            spread_send.at[k], spread_recv.at[k], spread_send_sem.at[k], spread_recv_sem.at[k], partner
        ).wait_send()
        others(back_send.at[k], back_send_sem.at[k], back_recv_sem.at[k, 0], n_view - 1).wait_send()
        others(back_send.at[k], sum_send_sem.at[k], back_recv_sem.at[k, 0], n_view - 1).wait_send()


def put_out(fine, coarse, fine_out, coarse_out, sem):
    copies = [
        pltpu.make_async_copy(src, dst, sem.at[i])
        for i, (src, dst) in enumerate([(coarse, coarse_out), (fine, fine_out)])
    ]
    for copy in copies:
        copy.start()
    for copy in copies:
        copy.wait()


def build(mesh, n_z, n_y):
    n_slab, n_view = mesh.shape["slab"], mesh.shape["view"]

    def body(*args):
        fine_volume, coarse_volume = args[0], args[1]
        rows_f, cells = fine_volume.shape
        rows_c = coarse_volume.shape[0]
        all_w = args[4].shape[2]
        rows_w = args[6].shape[0]
        width = cells // n_view
        tiles = width // 128
        anyspace = pl.BlockSpec(memory_space=pl.ANY)
        vmem = pl.BlockSpec(memory_space=pltpu.VMEM)
        dma = pltpu.SemaphoreType.DMA
        block = (tiles + 1, 16, 128)
        shapes = ((rows_f, cells), (rows_c, cells))
        results = pl.pallas_call(
            functools.partial(kernel, n_z, n_y, n_slab, n_view),
            name="sirt",
            out_shape=tuple(pltpu.VMEM(shape, F32) for shape in shapes),
            in_specs=[anyspace] * 12,
            out_specs=(vmem, vmem),
            scratch_shapes=[
                pltpu.VMEM((2, cells, 128), BF16),
                pltpu.VMEM((2, cells, 128), BF16),
                pltpu.VMEM(args[4].shape, BF16),
                pltpu.VMEM(args[5].shape, BF16),
                pltpu.VMEM(args[6].shape, F32),
                pltpu.VMEM(args[7].shape, F32),
                pltpu.SMEM(args[10].shape, jnp.int32),
                pltpu.SMEM(args[11].shape, jnp.int32),
                pltpu.VMEM((2, rows_f, cells), F32),
                pltpu.VMEM((n_view, 16, 128), F32),
                pltpu.VMEM((n_view, 16, 128), F32),
                pltpu.VMEM((rows_c, cells), F32),
                pltpu.VMEM((rows_c, cells), F32),
                pltpu.VMEM((2, 7, 8, 128), BF16),
                pltpu.VMEM((n_slab, 7, 8, 128), BF16),
                pltpu.VMEM((all_w, n_slab * 24), BF16),
                pltpu.VMEM((2, 24, all_w), BF16),
                pltpu.VMEM((n_slab * rows_w, 128), F32),
                pltpu.VMEM((n_slab * rows_w, 128), F32),
                pltpu.VMEM((ITERS, 2, 3, 8, 128), BF16),
                pltpu.VMEM((ITERS, n_slab, 3, 8, 128), BF16),
                pltpu.VMEM((ITERS, 3, 8, 128), BF16),
                pltpu.VMEM((ITERS, 3, 8, 128), BF16),
                pltpu.VMEM((n_view, 16, width + 128), F32),
                pltpu.VMEM((ITERS, n_view) + block, BF16),
                pltpu.VMEM((ITERS, n_view) + block, BF16),
                pltpu.VMEM((ITERS,) + block, BF16),
                pltpu.VMEM((ITERS, n_view) + block, BF16),
                dma((10 + 2 * n_view,)),
                dma((1,)),
                dma((1,)),
                dma((ITERS,)),
                dma((ITERS,)),
                dma((ITERS,)),
                dma((ITERS,)),
                dma((ITERS,)),
                dma((ITERS, n_view)),
                dma((ITERS,)),
                dma((ITERS, n_view)),
            ],
            compiler_params=pltpu.CompilerParams(collective_id=0, has_side_effects=True),
        )(*args)
        return pl.pallas_call(
            put_out,
            name="put_out",
            out_shape=tuple(jax.ShapeDtypeStruct(shape, F32) for shape in shapes),
            in_specs=[vmem, vmem],
            out_specs=(anyspace, anyspace),
            scratch_shapes=[dma((2,))],
        )(*(pltpu.with_memory_space_constraint(r, pltpu.VMEM) for r in results))

    return jax.shard_map(
        body,
        mesh=mesh,
        in_specs=(
            P("slab", None),
            P("slab", None),
            P("view", None, None),
            P("view", None, None),
            P("view", "slab", None),
            P("view", "slab", None),
            P("slab", "view", None),
            P("slab", "view", None),
            P("slab", None),
            P("slab", None),
            P("slab", None),
            P("view", "slab", None),
        ),
        out_specs=(P("slab", None), P("slab", None)),
        check_vma=False,
    )


def solution(mesh):
    return build(mesh, 8, 4)
```

```python
import functools

import jax
import jax.numpy as jnp
from jax import lax
from jax.experimental import pallas as pl
from jax.experimental.pallas import tpu as pltpu
from jax.sharding import PartitionSpec as P

ITERS = 3
BLOCK = 128
F32 = jnp.float32
BF16 = jnp.bfloat16


def dot(a, b):
    return lax.dot_general(a, b, (((1,), (0,)), ((), ())), preferred_element_type=F32)


def dot_nt(a, b):
    return lax.dot_general(a, b, (((1,), (1,)), ((), ())), preferred_element_type=F32)


def kernel(
    n_z,
    n_y,
    n_slab,
    n_view,
    fine_volume,
    coarse_volume,
    fine_rays,
    coarse_rays,
    fine_axial,
    coarse_axial,
    measured,
    ray_weight,
    fine_weight,
    coarse_weight,
    margin_blocks,
    ray_hits,
    fine_out,
    coarse_out,
    rays_f,
    rays_c,
    axial_f,
    axial_c,
    seen_in,
    weight_in,
    blocks,
    hits,
    vol_in,
    vol_f,
    wgt_f,
    vol_c,
    wgt_c,
    init_send,
    init_all,
    depth_t,
    depth_chip,
    depth_own,
    part_send,
    part_recv,
    rest_send,
    rest_recv,
    seen,
    weight,
    moment_send,
    moment_all,
    spread_send,
    spread_recv,
    back_own,
    back_send,
    back_recv,
    sum_send,
    sum_recv,
    load_sem,
    init_send_sem,
    init_recv_sem,
    first_send_sem,
    first_recv_sem,
    moment_send_sem,
    moment_recv_sem,
    spread_send_sem,
    spread_recv_sem,
    back_send_sem,
    back_recv_sem,
    sum_send_sem,
    sum_recv_sem,
):
    slab = lax.axis_index("slab")
    view = lax.axis_index("view")
    core = lax.rem(slab, 2)
    z = lax.rem(slab // 2, n_z)
    x_hi = slab // (2 * n_z)
    n_xhi = n_slab // (2 * n_z)
    y = lax.rem(view, n_y)
    x_lo = view // n_y
    n_xlo = n_view // n_y
    partner = slab + 1 - 2 * core
    cells = coarse_volume.shape[1]
    width = cells // n_view
    tiles = width // 128
    rows_f = fine_volume.shape[0]
    rows_w = measured.shape[0]
    all_w = fine_axial.shape[2]
    n_tile = ray_hits.shape[2]

    barrier = pltpu.get_barrier_semaphore()

    def greet_slab(i, carry):
        other = lax.rem(slab + 1 + i, n_slab)
        pl.semaphore_signal(barrier, inc=1, device_id={"slab": other}, device_id_type=pl.DeviceIdType.MESH)
        return carry

    def greet_view(i, carry):
        other = lax.rem(view + 1 + i, n_view)
        pl.semaphore_signal(barrier, inc=1, device_id={"view": other}, device_id_type=pl.DeviceIdType.MESH)
        return carry

    lax.fori_loop(0, n_slab - 1, greet_slab, 0)
    lax.fori_loop(0, n_view - 1, greet_view, 0)

    loads = []
    for i, (src, dst) in enumerate(
        [
            (ray_hits, hits),
            (fine_axial, axial_f),
            (coarse_axial, axial_c),
            (measured, seen_in),
            (ray_weight, weight_in),
            (margin_blocks, blocks),
            (coarse_volume, vol_c),
            (coarse_weight, wgt_c),
            (fine_volume, vol_in.at[0]),
            (fine_weight, vol_in.at[1]),
        ]
    ):
        copy = pltpu.make_async_copy(src, dst, load_sem.at[i])
        copy.start()
        loads.append(copy)
    ray_loads = []
    for b in range(n_view):
        part = pl.ds(b * width, width)
        pair = []
        for i, (src, dst) in enumerate([(coarse_rays, rays_c), (fine_rays, rays_f)]):
            copy = pltpu.make_async_copy(
                src.at[:, part, :], dst.at[:, part, :], load_sem.at[10 + 2 * b + i]
            )
            copy.start()
            pair.append(copy)
        ray_loads.append(pair)

    for copy in loads[:5]:
        copy.wait()
    half_w = all_w // 2
    row_tile = lax.broadcasted_iota(jnp.int32, (1, all_w), 1) // (all_w // n_tile)
    for v in range(2):
        hit = jnp.zeros((1, all_w), F32)
        for t in range(n_tile):
            hit = jnp.where(row_tile == t, hits[v, 0, t].astype(F32), hit)
        dc = (axial_c[v].astype(F32) * hit).astype(BF16)
        df = axial_f[v].astype(F32) * hit
        df = jnp.concatenate([df[:, :half_w], df[:, half_w:]], axis=0)
        init_send[v, 0] = dc[0:8, :half_w]
        init_send[v, 1] = dc[8:16, :half_w]
        init_send[v, 2] = dc[0:8, half_w:]
        init_send[v, 3] = dc[8:16, half_w:]
        init_send[v, 4] = df.astype(BF16)
        init_send[v, 5] = seen_in[:, v, :].astype(BF16)
        init_send[v, 6] = weight_in[:, v, :].astype(BF16)
    init_all[slab] = init_send[core]

    upper = lax.broadcasted_iota(jnp.int32, (8, 128), 0) >= rows_f

    def fine_half(packed, h):
        mine = upper if h else jnp.logical_not(upper)
        return jnp.where(mine, packed.astype(F32), 0.0).astype(BF16)

    for v in range(2):
        for h in range(2):
            depth = jnp.concatenate(
                [init_send[v, 2 * h], init_send[v, 2 * h + 1], fine_half(init_send[v, 4], h)], axis=0
            )
            depth_own[v, h * half_w : (h + 1) * half_w, :] = depth.T

    def chip_depth(i, index):
        for h in range(2):
            cols = slice(h * half_w, (h + 1) * half_w)
            depth_chip[i, 0:8, cols] = init_all[index, 2 * h]
            depth_chip[i, 8:16, cols] = init_all[index, 2 * h + 1]
            depth_chip[i, 16:24, cols] = fine_half(init_all[index, 4], h)

    chip_depth(0, slab)

    for copy in loads[5:]:
        copy.wait()
    block_id = lax.broadcasted_iota(jnp.int32, (1, cells), 1) // BLOCK
    keep = jnp.ones((1, cells), F32)
    for t in range(margin_blocks.shape[1]):
        keep = jnp.where(block_id == blocks[0, t], 0.0, keep)
    vol_c[...] = vol_c[...] * keep
    wgt_c[...] = wgt_c[...] * keep
    for b in range(n_view):
        for j in range(tiles):
            part = slice(b * width + j * 128, b * width + (j + 1) * 128)
            vol_f[b, j * rows_f : (j + 1) * rows_f, :] = vol_in[0, :, part]
            wgt_f[b, j * rows_f : (j + 1) * rows_f, :] = vol_in[1, :, part]

    group = lax.broadcasted_iota(jnp.int32, (16, 128), 0) // rows_f
    masks = [jnp.where(group == j, 1.0, 0.0).astype(F32) for j in range(tiles)]

    def add_moment(b, acc):
        part = pl.ds(pl.multiple_of(b * width, 128), width)
        lhs_c = vol_c[:, part].astype(BF16)
        packed = vol_f[b]
        lhs_f = jnp.concatenate([(packed * m).astype(BF16) for m in masks], axis=1)
        new = []
        for v in range(2):
            new.append(acc[v] + dot(lhs_c, rays_c[v, part, :]))
        for v in range(2):
            new.append(acc[2 + v] + dot(lhs_f, rays_f[v, part, :]))
        return new

    def finish_moment(k, acc):
        for v in range(2):
            mc = acc[v].astype(BF16)
            half = acc[2 + v][0:8] + acc[2 + v][8:16]
            whole = half + pltpu.roll(half, 4, 0)
            moment_send[k, v, 0] = mc[0:8]
            moment_send[k, v, 1] = mc[8:16]
            moment_send[k, v, 2] = whole.astype(BF16)
        if k > 0:
            moment_all[k, slab] = moment_send[k, core]

    zero = [jnp.zeros((16, 128), F32) for _ in range(4)]
    acc = zero
    for b in range(n_view):
        for copy in ray_loads[b]:
            copy.wait()
        acc = add_moment(b, acc)
    finish_moment(0, acc)
    for v in range(2):
        part = dot(depth_own[v], moment_send[0, v].reshape(24, 128)).astype(BF16)
        for i in range(n_slab):
            part_send[i, v] = part[i * rows_w : (i + 1) * rows_w]
    part_recv[slab] = part_send[slab]

    pl.semaphore_wait(barrier, n_slab + n_view - 2)

    def to_slab(src, dst, send_sem, recv_sem, other):
        return pltpu.make_async_remote_copy(
            src_ref=src,
            dst_ref=dst,
            send_sem=send_sem,
            recv_sem=recv_sem,
            device_id={"slab": other},
            device_id_type=pl.DeviceIdType.MESH,
        )

    n_chip = n_xhi * n_z

    def each_slab(send, first=0, last=n_chip - 1):
        def step(i, carry):
            turn = lax.rem(i, n_z)
            half = (turn + 1) // 2
            dz = n_z // 2 + half * (2 * lax.rem(turn, 2) - 1)
            dx = n_xhi - 1 - i // n_z
            chip = lax.rem(x_hi + dx, n_xhi) * n_z + lax.rem(z + dz + n_z, n_z)
            for c in range(2):
                send(2 * chip + c, c)
            return carry

        lax.fori_loop(first, last, step, 0)

    def send_init(other, c):
        to_slab(
            init_send.at[c], init_all.at[slab], init_send_sem.at[0], init_recv_sem.at[0], other
        ).start()

    def send_moments(k):
        def send(other, c):
            to_slab(
                moment_send.at[k, c],
                moment_all.at[k, slab],
                moment_send_sem.at[k],
                moment_recv_sem.at[k],
                other,
            ).start()

        each_slab(send)
        send(partner, 1 - core)

    def others(ref, sem_send, sem_recv, count):
        return pltpu.make_async_remote_copy(
            src_ref=ref.at[pl.ds(0, count)],
            dst_ref=ref.at[pl.ds(0, count)],
            send_sem=sem_send,
            recv_sem=sem_recv,
            device_id={"slab": partner},
            device_id_type=pl.DeviceIdType.MESH,
        )

    def send_part(other, c):
        to_slab(
            part_send.at[other],
            part_recv.at[slab],
            first_send_sem.at[0],
            first_recv_sem.at[0],
            other,
        ).start()

    def send_rest(other, c):
        to_slab(
            rest_send.at[c], rest_recv.at[slab], first_send_sem.at[1], first_recv_sem.at[1], other
        ).start()

    each_slab(send_part)
    send_part(partner, 1 - core)
    init_hand = to_slab(
        init_send.at[1 - core], init_all.at[slab], init_send_sem.at[1], init_recv_sem.at[1], partner
    )
    init_hand.start()
    init_hand.wait_recv()
    chip_depth(1, partner)
    others(part_recv, first_send_sem.at[0], first_recv_sem.at[0], n_slab - 1).wait_recv()
    summed = jnp.sum(part_recv[...].astype(F32), axis=0)
    for v in range(2):
        rest_send[v] = (weight_in[:, v, :] * (seen_in[:, v, :] - summed[v])).astype(BF16)
    rest_recv[slab] = rest_send[core]
    each_slab(send_rest)
    send_rest(partner, 1 - core)

    def finish_init():
        others(init_all, init_send_sem.at[0], init_recv_sem.at[0], n_slab - 2).wait_recv()
        for h in range(2):
            depth = jnp.concatenate(
                [init_all[:, 2 * h], init_all[:, 2 * h + 1], fine_half(init_all[:, 4], h)], axis=1
            )
            depth_t[h * half_w : (h + 1) * half_w, :] = depth.reshape(n_slab * 24, half_w).T
        seen[...] = init_all[:, 5].astype(F32).reshape(n_slab * rows_w, 128)
        weight[...] = init_all[:, 6].astype(F32).reshape(n_slab * rows_w, 128)

    view_order = sorted(
        [(dx, dy) for dx in range(n_xlo) for dy in range(n_y)],
        key=lambda p: -(p[0] + min(p[1], n_y - p[1])),
    )

    def view_of(step):
        dx, dy = step
        return lax.rem(x_lo + dx, n_xlo) * n_y + lax.rem(y + dy, n_y)

    def to_view(src, dst, send_sem, recv_sem, other):
        return pltpu.make_async_remote_copy(
            src_ref=src,
            dst_ref=dst,
            send_sem=send_sem,
            recv_sem=recv_sem,
            device_id={"view": other},
            device_id_type=pl.DeviceIdType.MESH,
        )

    for k in range(ITERS):
        if k == 0:
            others(rest_recv, first_send_sem.at[1], first_recv_sem.at[1], n_slab - 1).wait_recv()
            residual = rest_recv[...].reshape(n_slab * rows_w, 128)
            each_slab(send_init, n_chip - n_z, n_chip - 1)
        else:
            send_moments(k)
            if k == 1:
                finish_init()
            others(
                moment_all.at[k], moment_send_sem.at[k], moment_recv_sem.at[k], n_slab - 1
            ).wait_recv()
            projection = dot(depth_t[...], moment_all[k].reshape(n_slab * 24, 128))
            residual = (weight[...] * (seen[...] - projection)).astype(BF16)

        both = dot(depth_chip[...].reshape(48, all_w), residual)

        def spread_of(spread):
            fine = spread[16:24]
            return jnp.concatenate([spread[0:16], fine + pltpu.roll(fine, 4, 0)], axis=0).astype(BF16)

        spread_other = spread_of(both[24:48])
        for i in range(3):
            spread_send[k, i] = spread_other[8 * i : 8 * (i + 1)]
        hand = to_slab(
            spread_send.at[k], spread_recv.at[k], spread_send_sem.at[k], spread_recv_sem.at[k], partner
        )
        hand.start()
        spread_own = spread_of(both[0:24])

        def operands(spread):
            fine = spread[16:24].astype(F32)
            fine = jnp.concatenate([fine, fine], axis=0)
            return spread[0:16], [(fine * m).astype(BF16) for m in masks]

        def terms(coarse, fine, v, b):
            base = b * width
            part = pl.ds(pl.multiple_of(base, 128), width)
            term_c = dot_nt(coarse, rays_c[v, part, :])
            term_f = jnp.zeros((16, 128), F32)
            for j in range(tiles):
                piece = pl.ds(pl.multiple_of(base + j * 128, 128), 128)
                term_f = term_f + dot_nt(fine[j], rays_f[v, piece, :])
            return term_c, term_f

        own_c, own_f = operands(spread_own)
        for i, step in enumerate(view_order):
            term_c, term_f = terms(own_c, own_f, core, view_of(step))
            back_own[i, :, 0:width] = term_c
            back_own[i, :, width : width + 128] = term_f
        hand.wait_recv()
        other_c, other_f = operands(spread_recv[k].reshape(24, 128))
        for i, step in enumerate(view_order):
            b = view_of(step)
            term_c, term_f = terms(other_c, other_f, 1 - core, b)
            term_c = term_c + back_own[i, :, 0:width]
            term_f = term_f + back_own[i, :, width : width + 128]
            dest = back_recv.at[k, view] if step == (0, 0) else back_send.at[k, b]
            for j in range(tiles):
                dest[j] = term_c[:, j * 128 : (j + 1) * 128].astype(BF16)
            dest[tiles] = term_f.astype(BF16)
            if step != (0, 0):
                to_view(
                    back_send.at[k, b],
                    back_recv.at[k, view],
                    back_send_sem.at[k],
                    back_recv_sem.at[k, view],
                    b,
                ).start()
        if k == 0:
            each_slab(send_init, 0, n_chip - n_z)
        total = back_recv[k, view].astype(F32)
        for step in reversed(view_order):
            if step == (0, 0):
                continue
            b = view_of(step)
            to_view(
                back_send.at[k, b], back_recv.at[k, b], back_send_sem.at[k], back_recv_sem.at[k, b], b
            ).wait_recv()
            total = total + back_recv[k, b].astype(F32)
        sum_send[k] = total.astype(BF16)
        for step in view_order:
            if step == (0, 0):
                continue
            to_view(
                sum_send.at[k],
                sum_recv.at[k, view],
                sum_send_sem.at[k],
                sum_recv_sem.at[k, view],
                view_of(step),
            ).start()
        acc = zero
        for step in reversed(view_order):
            b = view_of(step)
            if step == (0, 0):
                back = sum_send[k].astype(F32)
            else:
                to_view(
                    sum_send.at[k], sum_recv.at[k, b], sum_send_sem.at[k], sum_recv_sem.at[k, b], b
                ).wait_recv()
                back = sum_recv[k, b].astype(F32)
            for j in range(tiles):
                piece = pl.ds(pl.multiple_of(b * width + j * 128, 128), 128)
                vol_c[:, piece] = vol_c[:, piece] + wgt_c[:, piece] * back[j]
            vol_f[b] = vol_f[b] + wgt_f[b] * back[tiles]
            if k < ITERS - 1:
                acc = add_moment(b, acc)
        if k < ITERS - 1:
            finish_moment(k + 1, acc)

    coarse_out[...] = vol_c[...]
    for b in range(n_view):
        for j in range(tiles):
            part = slice(b * width + j * 128, b * width + (j + 1) * 128)
            fine_out[:, part] = vol_f[b, j * rows_f : (j + 1) * rows_f, :]

    others(init_all, init_send_sem.at[0], init_recv_sem.at[0], n_slab - 2).wait_send()
    init_hand.wait_send()
    others(part_recv, first_send_sem.at[0], first_recv_sem.at[0], n_slab - 1).wait_send()
    others(rest_recv, first_send_sem.at[1], first_recv_sem.at[1], n_slab - 1).wait_send()
    for k in range(ITERS):
        if k > 0:
            others(
                moment_all.at[k], moment_send_sem.at[k], moment_recv_sem.at[k], n_slab - 1
            ).wait_send()
        to_slab(
            spread_send.at[k], spread_recv.at[k], spread_send_sem.at[k], spread_recv_sem.at[k], partner
        ).wait_send()
        others(back_send.at[k], back_send_sem.at[k], back_recv_sem.at[k, 0], n_view - 1).wait_send()
        others(back_send.at[k], sum_send_sem.at[k], back_recv_sem.at[k, 0], n_view - 1).wait_send()


def put_out(fine, coarse, fine_out, coarse_out, sem):
    copies = [
        pltpu.make_async_copy(src, dst, sem.at[i])
        for i, (src, dst) in enumerate([(coarse, coarse_out), (fine, fine_out)])
    ]
    for copy in copies:
        copy.start()
    for copy in copies:
        copy.wait()


def build(mesh, n_z, n_y):
    n_slab, n_view = mesh.shape["slab"], mesh.shape["view"]

    def body(*args):
        fine_volume, coarse_volume = args[0], args[1]
        rows_f, cells = fine_volume.shape
        rows_c = coarse_volume.shape[0]
        all_w = args[4].shape[2]
        rows_w = args[6].shape[0]
        width = cells // n_view
        tiles = width // 128
        anyspace = pl.BlockSpec(memory_space=pl.ANY)
        vmem = pl.BlockSpec(memory_space=pltpu.VMEM)
        dma = pltpu.SemaphoreType.DMA
        block = (tiles + 1, 16, 128)
        shapes = ((rows_f, cells), (rows_c, cells))
        results = pl.pallas_call(
            functools.partial(kernel, n_z, n_y, n_slab, n_view),
            name="sirt",
            out_shape=tuple(pltpu.VMEM(shape, F32) for shape in shapes),
            in_specs=[anyspace] * 12,
            out_specs=(vmem, vmem),
            scratch_shapes=[
                pltpu.VMEM((2, cells, 128), BF16),
                pltpu.VMEM((2, cells, 128), BF16),
                pltpu.VMEM(args[4].shape, BF16),
                pltpu.VMEM(args[5].shape, BF16),
                pltpu.VMEM(args[6].shape, F32),
                pltpu.VMEM(args[7].shape, F32),
                pltpu.SMEM(args[10].shape, jnp.int32),
                pltpu.SMEM(args[11].shape, jnp.int32),
                pltpu.VMEM((2, rows_f, cells), F32),
                pltpu.VMEM((n_view, 16, 128), F32),
                pltpu.VMEM((n_view, 16, 128), F32),
                pltpu.VMEM((rows_c, cells), F32),
                pltpu.VMEM((rows_c, cells), F32),
                pltpu.VMEM((2, 7, 8, 128), BF16),
                pltpu.VMEM((n_slab, 7, 8, 128), BF16),
                pltpu.VMEM((all_w, n_slab * 24), BF16),
                pltpu.VMEM((2, 24, all_w), BF16),
                pltpu.VMEM((2, all_w, 24), BF16),
                pltpu.VMEM((n_slab, 2, rows_w, 128), BF16),
                pltpu.VMEM((n_slab, 2, rows_w, 128), BF16),
                pltpu.VMEM((2, rows_w, 128), BF16),
                pltpu.VMEM((n_slab, rows_w, 128), BF16),
                pltpu.VMEM((n_slab * rows_w, 128), F32),
                pltpu.VMEM((n_slab * rows_w, 128), F32),
                pltpu.VMEM((ITERS, 2, 3, 8, 128), BF16),
                pltpu.VMEM((ITERS, n_slab, 3, 8, 128), BF16),
                pltpu.VMEM((ITERS, 3, 8, 128), BF16),
                pltpu.VMEM((ITERS, 3, 8, 128), BF16),
                pltpu.VMEM((n_view, 16, width + 128), F32),
                pltpu.VMEM((ITERS, n_view) + block, BF16),
                pltpu.VMEM((ITERS, n_view) + block, BF16),
                pltpu.VMEM((ITERS,) + block, BF16),
                pltpu.VMEM((ITERS, n_view) + block, BF16),
                dma((10 + 2 * n_view,)),
                dma((2,)),
                dma((2,)),
                dma((2,)),
                dma((2,)),
                dma((ITERS,)),
                dma((ITERS,)),
                dma((ITERS,)),
                dma((ITERS,)),
                dma((ITERS,)),
                dma((ITERS, n_view)),
                dma((ITERS,)),
                dma((ITERS, n_view)),
            ],
            compiler_params=pltpu.CompilerParams(collective_id=0, has_side_effects=True),
        )(*args)
        return pl.pallas_call(
            put_out,
            name="put_out",
            out_shape=tuple(jax.ShapeDtypeStruct(shape, F32) for shape in shapes),
            in_specs=[vmem, vmem],
            out_specs=(anyspace, anyspace),
            scratch_shapes=[dma((2,))],
        )(*(pltpu.with_memory_space_constraint(r, pltpu.VMEM) for r in results))

    return jax.shard_map(
        body,
        mesh=mesh,
        in_specs=(
            P("slab", None),
            P("slab", None),
            P("view", None, None),
            P("view", None, None),
            P("view", "slab", None),
            P("view", "slab", None),
            P("slab", "view", None),
            P("slab", "view", None),
            P("slab", None),
            P("slab", None),
            P("slab", None),
            P("view", "slab", None),
        ),
        out_specs=(P("slab", None), P("slab", None)),
        check_vma=False,
    )


def solution(mesh):
    return build(mesh, 8, 4)
```

```python
import functools

import jax
import jax.numpy as jnp
from jax import lax
from jax.experimental import pallas as pl
from jax.experimental.pallas import tpu as pltpu
from jax.sharding import PartitionSpec as P

ITERS = 3
BLOCK = 128
F32 = jnp.float32
BF16 = jnp.bfloat16


def dot(a, b):
    return lax.dot_general(a, b, (((1,), (0,)), ((), ())), preferred_element_type=F32)


def dot_nt(a, b):
    return lax.dot_general(a, b, (((1,), (1,)), ((), ())), preferred_element_type=F32)


def kernel(
    n_z,
    n_y,
    n_slab,
    n_view,
    fine_volume,
    coarse_volume,
    fine_rays,
    coarse_rays,
    fine_axial,
    coarse_axial,
    measured,
    ray_weight,
    fine_weight,
    coarse_weight,
    margin_blocks,
    ray_hits,
    fine_out,
    coarse_out,
    rays_f,
    rays_c,
    axial_f,
    axial_c,
    seen_in,
    weight_in,
    blocks,
    hits,
    vol_in,
    vol_f,
    wgt_f,
    vol_c,
    wgt_c,
    init_send,
    init_all,
    depth_t,
    depth_chip,
    depth_own,
    part_send,
    part_recv,
    rest_send,
    rest_recv,
    seen,
    weight,
    moment_send,
    moment_all,
    spread_send,
    spread_recv,
    back_own,
    back_send,
    back_recv,
    sum_send,
    sum_recv,
    load_sem,
    init_send_sem,
    init_recv_sem,
    first_send_sem,
    first_recv_sem,
    moment_send_sem,
    moment_recv_sem,
    spread_send_sem,
    spread_recv_sem,
    back_send_sem,
    back_recv_sem,
    sum_send_sem,
    sum_recv_sem,
):
    slab = lax.axis_index("slab")
    view = lax.axis_index("view")
    core = lax.rem(slab, 2)
    z = lax.rem(slab // 2, n_z)
    x_hi = slab // (2 * n_z)
    n_xhi = n_slab // (2 * n_z)
    y = lax.rem(view, n_y)
    x_lo = view // n_y
    n_xlo = n_view // n_y
    partner = slab + 1 - 2 * core
    cells = coarse_volume.shape[1]
    width = cells // n_view
    tiles = width // 128
    rows_f = fine_volume.shape[0]
    rows_w = measured.shape[0]
    all_w = fine_axial.shape[2]
    n_tile = ray_hits.shape[2]

    barrier = pltpu.get_barrier_semaphore()

    def greet_slab(i, carry):
        other = lax.rem(slab + 1 + i, n_slab)
        pl.semaphore_signal(barrier, inc=1, device_id={"slab": other}, device_id_type=pl.DeviceIdType.MESH)
        return carry

    def greet_view(i, carry):
        other = lax.rem(view + 1 + i, n_view)
        pl.semaphore_signal(barrier, inc=1, device_id={"view": other}, device_id_type=pl.DeviceIdType.MESH)
        return carry

    lax.fori_loop(0, n_slab - 1, greet_slab, 0)
    lax.fori_loop(0, n_view - 1, greet_view, 0)

    loads = []
    for i, (src, dst) in enumerate(
        [
            (ray_hits, hits),
            (fine_axial, axial_f),
            (coarse_axial, axial_c),
            (measured, seen_in),
            (ray_weight, weight_in),
            (margin_blocks, blocks),
            (coarse_volume, vol_c),
            (coarse_weight, wgt_c),
            (fine_volume, vol_in.at[0]),
            (fine_weight, vol_in.at[1]),
        ]
    ):
        copy = pltpu.make_async_copy(src, dst, load_sem.at[i])
        copy.start()
        loads.append(copy)
    ray_loads = []
    for b in range(n_view):
        part = pl.ds(b * width, width)
        pair = []
        for i, (src, dst) in enumerate([(coarse_rays, rays_c), (fine_rays, rays_f)]):
            copy = pltpu.make_async_copy(
                src.at[:, part, :], dst.at[:, part, :], load_sem.at[10 + 2 * b + i]
            )
            copy.start()
            pair.append(copy)
        ray_loads.append(pair)

    for copy in loads[:5]:
        copy.wait()
    half_w = all_w // 2
    row_tile = lax.broadcasted_iota(jnp.int32, (1, all_w), 1) // (all_w // n_tile)
    for v in range(2):
        hit = jnp.zeros((1, all_w), F32)
        for t in range(n_tile):
            hit = jnp.where(row_tile == t, hits[v, 0, t].astype(F32), hit)
        dc = (axial_c[v].astype(F32) * hit).astype(BF16)
        df = axial_f[v].astype(F32) * hit
        df = jnp.concatenate([df[:, :half_w], df[:, half_w:]], axis=0)
        init_send[v, 0] = dc[0:8, :half_w]
        init_send[v, 1] = dc[8:16, :half_w]
        init_send[v, 2] = dc[0:8, half_w:]
        init_send[v, 3] = dc[8:16, half_w:]
        init_send[v, 4] = df.astype(BF16)
        init_send[v, 5] = seen_in[:, v, :].astype(BF16)
        init_send[v, 6] = weight_in[:, v, :].astype(BF16)
    init_all[slab] = init_send[core]

    upper = lax.broadcasted_iota(jnp.int32, (8, 128), 0) >= rows_f

    def fine_half(packed, h):
        mine = upper if h else jnp.logical_not(upper)
        return jnp.where(mine, packed.astype(F32), 0.0).astype(BF16)

    for v in range(2):
        for h in range(2):
            depth = jnp.concatenate(
                [init_send[v, 2 * h], init_send[v, 2 * h + 1], fine_half(init_send[v, 4], h)], axis=0
            )
            depth_own[v, h * half_w : (h + 1) * half_w, :] = depth.T

    def chip_depth(i, index):
        for h in range(2):
            cols = slice(h * half_w, (h + 1) * half_w)
            depth_chip[i, 0:8, cols] = init_all[index, 2 * h]
            depth_chip[i, 8:16, cols] = init_all[index, 2 * h + 1]
            depth_chip[i, 16:24, cols] = fine_half(init_all[index, 4], h)

    chip_depth(0, slab)

    for copy in loads[5:]:
        copy.wait()
    block_id = lax.broadcasted_iota(jnp.int32, (1, cells), 1) // BLOCK
    keep = jnp.ones((1, cells), F32)
    for t in range(margin_blocks.shape[1]):
        keep = jnp.where(block_id == blocks[0, t], 0.0, keep)
    vol_c[...] = vol_c[...] * keep
    wgt_c[...] = wgt_c[...] * keep
    for b in range(n_view):
        for j in range(tiles):
            part = slice(b * width + j * 128, b * width + (j + 1) * 128)
            vol_f[b, j * rows_f : (j + 1) * rows_f, :] = vol_in[0, :, part]
            wgt_f[b, j * rows_f : (j + 1) * rows_f, :] = vol_in[1, :, part]

    group = lax.broadcasted_iota(jnp.int32, (16, 128), 0) // rows_f
    masks = [jnp.where(group == j, 1.0, 0.0).astype(F32) for j in range(tiles)]

    def add_moment(b, acc):
        part = pl.ds(pl.multiple_of(b * width, 128), width)
        lhs_c = vol_c[:, part].astype(BF16)
        packed = vol_f[b]
        lhs_f = jnp.concatenate([(packed * m).astype(BF16) for m in masks], axis=1)
        new = []
        for v in range(2):
            new.append(acc[v] + dot(lhs_c, rays_c[v, part, :]))
        for v in range(2):
            new.append(acc[2 + v] + dot(lhs_f, rays_f[v, part, :]))
        return new

    def finish_moment(k, acc):
        for v in range(2):
            mc = acc[v].astype(BF16)
            half = acc[2 + v][0:8] + acc[2 + v][8:16]
            whole = half + pltpu.roll(half, 4, 0)
            moment_send[k, v, 0] = mc[0:8]
            moment_send[k, v, 1] = mc[8:16]
            moment_send[k, v, 2] = whole.astype(BF16)
        if k > 0:
            moment_all[k, slab] = moment_send[k, core]

    zero = [jnp.zeros((16, 128), F32) for _ in range(4)]
    acc = zero
    for b in range(n_view):
        for copy in ray_loads[b]:
            copy.wait()
        acc = add_moment(b, acc)
    finish_moment(0, acc)
    for v in range(2):
        part = dot(depth_own[v], moment_send[0, v].reshape(24, 128)).astype(BF16)
        for i in range(n_slab):
            part_send[i, v] = part[i * rows_w : (i + 1) * rows_w]
    part_recv[slab] = part_send[slab]

    pl.semaphore_wait(barrier, n_slab + n_view - 2)

    def to_slab(src, dst, send_sem, recv_sem, other):
        return pltpu.make_async_remote_copy(
            src_ref=src,
            dst_ref=dst,
            send_sem=send_sem,
            recv_sem=recv_sem,
            device_id={"slab": other},
            device_id_type=pl.DeviceIdType.MESH,
        )

    n_chip = n_xhi * n_z

    def each_slab(send, first=0, last=n_chip - 1):
        def step(i, carry):
            turn = lax.rem(i, n_z)
            half = (turn + 1) // 2
            dz = n_z // 2 + half * (2 * lax.rem(turn, 2) - 1)
            dx = n_xhi - 1 - i // n_z
            chip = lax.rem(x_hi + dx, n_xhi) * n_z + lax.rem(z + dz + n_z, n_z)
            for c in range(2):
                send(2 * chip + c, c)
            return carry

        lax.fori_loop(first, last, step, 0)

    def send_init(other, c):
        to_slab(
            init_send.at[c], init_all.at[slab], init_send_sem.at[0], init_recv_sem.at[0], other
        ).start()

    def send_moments(k):
        def send(other, c):
            to_slab(
                moment_send.at[k, c],
                moment_all.at[k, slab],
                moment_send_sem.at[k],
                moment_recv_sem.at[k],
                other,
            ).start()

        each_slab(send)
        send(partner, 1 - core)

    def others(ref, sem_send, sem_recv, count):
        return pltpu.make_async_remote_copy(
            src_ref=ref.at[pl.ds(0, count)],
            dst_ref=ref.at[pl.ds(0, count)],
            send_sem=sem_send,
            recv_sem=sem_recv,
            device_id={"slab": partner},
            device_id_type=pl.DeviceIdType.MESH,
        )

    def send_part(other, c):
        to_slab(
            part_send.at[other],
            part_recv.at[slab],
            first_send_sem.at[0],
            first_recv_sem.at[0],
            other,
        ).start()

    def send_rest(other, c):
        to_slab(
            rest_send.at[c], rest_recv.at[slab], first_send_sem.at[1], first_recv_sem.at[1], other
        ).start()

    each_slab(send_part)
    send_part(partner, 1 - core)
    init_hand = to_slab(
        init_send.at[1 - core], init_all.at[slab], init_send_sem.at[1], init_recv_sem.at[1], partner
    )
    init_hand.start()
    init_hand.wait_recv()
    chip_depth(1, partner)
    others(part_recv, first_send_sem.at[0], first_recv_sem.at[0], n_slab - 1).wait_recv()
    summed = jnp.sum(part_recv[...].astype(F32), axis=0)
    for v in range(2):
        rest_send[v] = (weight_in[:, v, :] * (seen_in[:, v, :] - summed[v])).astype(BF16)
    rest_recv[slab] = rest_send[core]
    each_slab(send_rest)
    send_rest(partner, 1 - core)
    each_slab(send_init, 0, n_chip - n_z)

    def finish_init():
        others(init_all, init_send_sem.at[0], init_recv_sem.at[0], n_slab - 2).wait_recv()
        for h in range(2):
            depth = jnp.concatenate(
                [init_all[:, 2 * h], init_all[:, 2 * h + 1], fine_half(init_all[:, 4], h)], axis=1
            )
            depth_t[h * half_w : (h + 1) * half_w, :] = depth.reshape(n_slab * 24, half_w).T
        seen[...] = init_all[:, 5].astype(F32).reshape(n_slab * rows_w, 128)
        weight[...] = init_all[:, 6].astype(F32).reshape(n_slab * rows_w, 128)

    view_order = sorted(
        [(dx, dy) for dx in range(n_xlo) for dy in range(n_y)],
        key=lambda p: -(p[0] + min(p[1], n_y - p[1])),
    )

    def view_of(step):
        dx, dy = step
        return lax.rem(x_lo + dx, n_xlo) * n_y + lax.rem(y + dy, n_y)

    def to_view(src, dst, send_sem, recv_sem, other):
        return pltpu.make_async_remote_copy(
            src_ref=src,
            dst_ref=dst,
            send_sem=send_sem,
            recv_sem=recv_sem,
            device_id={"view": other},
            device_id_type=pl.DeviceIdType.MESH,
        )

    for k in range(ITERS):
        if k == 0:
            others(rest_recv, first_send_sem.at[1], first_recv_sem.at[1], n_slab - 1).wait_recv()
            residual = rest_recv[...].reshape(n_slab * rows_w, 128)
        else:
            send_moments(k)
            if k == 1:
                finish_init()
            others(
                moment_all.at[k], moment_send_sem.at[k], moment_recv_sem.at[k], n_slab - 1
            ).wait_recv()
            projection = dot(depth_t[...], moment_all[k].reshape(n_slab * 24, 128))
            residual = (weight[...] * (seen[...] - projection)).astype(BF16)

        both = dot(depth_chip[...].reshape(48, all_w), residual)

        def spread_of(spread):
            fine = spread[16:24]
            return jnp.concatenate([spread[0:16], fine + pltpu.roll(fine, 4, 0)], axis=0).astype(BF16)

        spread_other = spread_of(both[24:48])
        for i in range(3):
            spread_send[k, i] = spread_other[8 * i : 8 * (i + 1)]
        hand = to_slab(
            spread_send.at[k], spread_recv.at[k], spread_send_sem.at[k], spread_recv_sem.at[k], partner
        )
        hand.start()
        if k == 0:
            each_slab(send_init, n_chip - n_z, n_chip - 1)
        spread_own = spread_of(both[0:24])

        def operands(spread):
            fine = spread[16:24].astype(F32)
            fine = jnp.concatenate([fine, fine], axis=0)
            return spread[0:16], [(fine * m).astype(BF16) for m in masks]

        def terms(coarse, fine, v, b):
            base = b * width
            part = pl.ds(pl.multiple_of(base, 128), width)
            term_c = dot_nt(coarse, rays_c[v, part, :])
            term_f = jnp.zeros((16, 128), F32)
            for j in range(tiles):
                piece = pl.ds(pl.multiple_of(base + j * 128, 128), 128)
                term_f = term_f + dot_nt(fine[j], rays_f[v, piece, :])
            return term_c, term_f

        own_c, own_f = operands(spread_own)
        for i, step in enumerate(view_order):
            term_c, term_f = terms(own_c, own_f, core, view_of(step))
            back_own[i, :, 0:width] = term_c
            back_own[i, :, width : width + 128] = term_f
        hand.wait_recv()
        other_c, other_f = operands(spread_recv[k].reshape(24, 128))
        for i, step in enumerate(view_order):
            b = view_of(step)
            term_c, term_f = terms(other_c, other_f, 1 - core, b)
            term_c = term_c + back_own[i, :, 0:width]
            term_f = term_f + back_own[i, :, width : width + 128]
            dest = back_recv.at[k, view] if step == (0, 0) else back_send.at[k, b]
            for j in range(tiles):
                dest[j] = term_c[:, j * 128 : (j + 1) * 128].astype(BF16)
            dest[tiles] = term_f.astype(BF16)
            if step != (0, 0):
                to_view(
                    back_send.at[k, b],
                    back_recv.at[k, view],
                    back_send_sem.at[k],
                    back_recv_sem.at[k, view],
                    b,
                ).start()
        total = back_recv[k, view].astype(F32)
        for step in reversed(view_order):
            if step == (0, 0):
                continue
            b = view_of(step)
            to_view(
                back_send.at[k, b], back_recv.at[k, b], back_send_sem.at[k], back_recv_sem.at[k, b], b
            ).wait_recv()
            total = total + back_recv[k, b].astype(F32)
        sum_send[k] = total.astype(BF16)
        for step in view_order:
            if step == (0, 0):
                continue
            to_view(
                sum_send.at[k],
                sum_recv.at[k, view],
                sum_send_sem.at[k],
                sum_recv_sem.at[k, view],
                view_of(step),
            ).start()
        acc = zero
        for step in reversed(view_order):
            b = view_of(step)
            if step == (0, 0):
                back = sum_send[k].astype(F32)
            else:
                to_view(
                    sum_send.at[k], sum_recv.at[k, b], sum_send_sem.at[k], sum_recv_sem.at[k, b], b
                ).wait_recv()
                back = sum_recv[k, b].astype(F32)
            for j in range(tiles):
                piece = pl.ds(pl.multiple_of(b * width + j * 128, 128), 128)
                vol_c[:, piece] = vol_c[:, piece] + wgt_c[:, piece] * back[j]
            vol_f[b] = vol_f[b] + wgt_f[b] * back[tiles]
            if k < ITERS - 1:
                acc = add_moment(b, acc)
        if k < ITERS - 1:
            finish_moment(k + 1, acc)

    coarse_out[...] = vol_c[...]
    for b in range(n_view):
        for j in range(tiles):
            part = slice(b * width + j * 128, b * width + (j + 1) * 128)
            fine_out[:, part] = vol_f[b, j * rows_f : (j + 1) * rows_f, :]

    others(init_all, init_send_sem.at[0], init_recv_sem.at[0], n_slab - 2).wait_send()
    init_hand.wait_send()
    others(part_recv, first_send_sem.at[0], first_recv_sem.at[0], n_slab - 1).wait_send()
    others(rest_recv, first_send_sem.at[1], first_recv_sem.at[1], n_slab - 1).wait_send()
    for k in range(ITERS):
        if k > 0:
            others(
                moment_all.at[k], moment_send_sem.at[k], moment_recv_sem.at[k], n_slab - 1
            ).wait_send()
        to_slab(
            spread_send.at[k], spread_recv.at[k], spread_send_sem.at[k], spread_recv_sem.at[k], partner
        ).wait_send()
        others(back_send.at[k], back_send_sem.at[k], back_recv_sem.at[k, 0], n_view - 1).wait_send()
        others(back_send.at[k], sum_send_sem.at[k], back_recv_sem.at[k, 0], n_view - 1).wait_send()


def put_out(fine, coarse, fine_out, coarse_out, sem):
    copies = [
        pltpu.make_async_copy(src, dst, sem.at[i])
        for i, (src, dst) in enumerate([(coarse, coarse_out), (fine, fine_out)])
    ]
    for copy in copies:
        copy.start()
    for copy in copies:
        copy.wait()


def build(mesh, n_z, n_y):
    n_slab, n_view = mesh.shape["slab"], mesh.shape["view"]

    def body(*args):
        fine_volume, coarse_volume = args[0], args[1]
        rows_f, cells = fine_volume.shape
        rows_c = coarse_volume.shape[0]
        all_w = args[4].shape[2]
        rows_w = args[6].shape[0]
        width = cells // n_view
        tiles = width // 128
        anyspace = pl.BlockSpec(memory_space=pl.ANY)
        vmem = pl.BlockSpec(memory_space=pltpu.VMEM)
        dma = pltpu.SemaphoreType.DMA
        block = (tiles + 1, 16, 128)
        shapes = ((rows_f, cells), (rows_c, cells))
        results = pl.pallas_call(
            functools.partial(kernel, n_z, n_y, n_slab, n_view),
            name="sirt",
            out_shape=tuple(pltpu.VMEM(shape, F32) for shape in shapes),
            in_specs=[anyspace] * 12,
            out_specs=(vmem, vmem),
            scratch_shapes=[
                pltpu.VMEM((2, cells, 128), BF16),
                pltpu.VMEM((2, cells, 128), BF16),
                pltpu.VMEM(args[4].shape, BF16),
                pltpu.VMEM(args[5].shape, BF16),
                pltpu.VMEM(args[6].shape, F32),
                pltpu.VMEM(args[7].shape, F32),
                pltpu.SMEM(args[10].shape, jnp.int32),
                pltpu.SMEM(args[11].shape, jnp.int32),
                pltpu.VMEM((2, rows_f, cells), F32),
                pltpu.VMEM((n_view, 16, 128), F32),
                pltpu.VMEM((n_view, 16, 128), F32),
                pltpu.VMEM((rows_c, cells), F32),
                pltpu.VMEM((rows_c, cells), F32),
                pltpu.VMEM((2, 7, 8, 128), BF16),
                pltpu.VMEM((n_slab, 7, 8, 128), BF16),
                pltpu.VMEM((all_w, n_slab * 24), BF16),
                pltpu.VMEM((2, 24, all_w), BF16),
                pltpu.VMEM((2, all_w, 24), BF16),
                pltpu.VMEM((n_slab, 2, rows_w, 128), BF16),
                pltpu.VMEM((n_slab, 2, rows_w, 128), BF16),
                pltpu.VMEM((2, rows_w, 128), BF16),
                pltpu.VMEM((n_slab, rows_w, 128), BF16),
                pltpu.VMEM((n_slab * rows_w, 128), F32),
                pltpu.VMEM((n_slab * rows_w, 128), F32),
                pltpu.VMEM((ITERS, 2, 3, 8, 128), BF16),
                pltpu.VMEM((ITERS, n_slab, 3, 8, 128), BF16),
                pltpu.VMEM((ITERS, 3, 8, 128), BF16),
                pltpu.VMEM((ITERS, 3, 8, 128), BF16),
                pltpu.VMEM((n_view, 16, width + 128), F32),
                pltpu.VMEM((ITERS, n_view) + block, BF16),
                pltpu.VMEM((ITERS, n_view) + block, BF16),
                pltpu.VMEM((ITERS,) + block, BF16),
                pltpu.VMEM((ITERS, n_view) + block, BF16),
                dma((10 + 2 * n_view,)),
                dma((2,)),
                dma((2,)),
                dma((2,)),
                dma((2,)),
                dma((ITERS,)),
                dma((ITERS,)),
                dma((ITERS,)),
                dma((ITERS,)),
                dma((ITERS,)),
                dma((ITERS, n_view)),
                dma((ITERS,)),
                dma((ITERS, n_view)),
            ],
            compiler_params=pltpu.CompilerParams(collective_id=0, has_side_effects=True),
        )(*args)
        return pl.pallas_call(
            put_out,
            name="put_out",
            out_shape=tuple(jax.ShapeDtypeStruct(shape, F32) for shape in shapes),
            in_specs=[vmem, vmem],
            out_specs=(anyspace, anyspace),
            scratch_shapes=[dma((2,))],
        )(*(pltpu.with_memory_space_constraint(r, pltpu.VMEM) for r in results))

    return jax.shard_map(
        body,
        mesh=mesh,
        in_specs=(
            P("slab", None),
            P("slab", None),
            P("view", None, None),
            P("view", None, None),
            P("view", "slab", None),
            P("view", "slab", None),
            P("slab", "view", None),
            P("slab", "view", None),
            P("slab", None),
            P("slab", None),
            P("slab", None),
            P("view", "slab", None),
        ),
        out_specs=(P("slab", None), P("slab", None)),
        check_vma=False,
    )


def solution(mesh):
    return build(mesh, 8, 4)
```

```python
import functools

import jax
import jax.numpy as jnp
from jax import lax
from jax.experimental import pallas as pl
from jax.experimental.pallas import tpu as pltpu
from jax.sharding import PartitionSpec as P

ITERS = 3
BLOCK = 128
F32 = jnp.float32
BF16 = jnp.bfloat16


def dot(a, b):
    return lax.dot_general(a, b, (((1,), (0,)), ((), ())), preferred_element_type=F32)


def dot_nt(a, b):
    return lax.dot_general(a, b, (((1,), (1,)), ((), ())), preferred_element_type=F32)


def kernel(
    n_z,
    n_y,
    n_slab,
    n_view,
    fine_volume,
    coarse_volume,
    fine_rays,
    coarse_rays,
    fine_axial,
    coarse_axial,
    measured,
    ray_weight,
    fine_weight,
    coarse_weight,
    margin_blocks,
    ray_hits,
    fine_out,
    coarse_out,
    rays_f,
    rays_c,
    axial_f,
    axial_c,
    seen_in,
    weight_in,
    blocks,
    hits,
    vol_in,
    vol_f,
    wgt_f,
    wgt_c,
    init_send,
    init_all,
    depth_t,
    depth_chip,
    depth_own,
    part_send,
    part_recv,
    rest_send,
    rest_recv,
    seen,
    weight,
    moment_send,
    moment_all,
    spread_send,
    spread_recv,
    back_own,
    back_send,
    back_recv,
    sum_send,
    sum_recv,
    load_sem,
    init_send_sem,
    init_recv_sem,
    first_send_sem,
    first_recv_sem,
    moment_send_sem,
    moment_recv_sem,
    spread_send_sem,
    spread_recv_sem,
    back_send_sem,
    back_recv_sem,
    sum_send_sem,
    sum_recv_sem,
):
    slab = lax.axis_index("slab")
    view = lax.axis_index("view")
    core = lax.rem(slab, 2)
    z = lax.rem(slab // 2, n_z)
    x_hi = slab // (2 * n_z)
    n_xhi = n_slab // (2 * n_z)
    y = lax.rem(view, n_y)
    x_lo = view // n_y
    n_xlo = n_view // n_y
    partner = slab + 1 - 2 * core
    vol_c = coarse_out
    cells = coarse_volume.shape[1]
    width = cells // n_view
    tiles = width // 128
    rows_f = fine_volume.shape[0]
    rows_w = measured.shape[0]
    all_w = fine_axial.shape[2]
    n_tile = ray_hits.shape[2]

    barrier = pltpu.get_barrier_semaphore()

    along_z = sorted(range(n_z), key=lambda dz: -min(dz, n_z - dz))
    far_chips = [(dx, dz) for dx in range(n_xhi - 1, 0, -1) for dz in along_z]
    near_chips = [(0, dz) for dz in along_z if dz]

    def each_slab(send, chips=far_chips + near_chips):
        for dx, dz in chips:
            chip = lax.rem(x_hi + dx, n_xhi) * n_z + lax.rem(z + dz, n_z)
            for c in range(2):
                send(2 * chip + c, c, dx)

    def greet(other, c, dx):
        pl.semaphore_signal(barrier, inc=1, device_id={"slab": other}, device_id_type=pl.DeviceIdType.MESH)

    def greet_view(i, carry):
        other = lax.rem(view + 1 + i, n_view)
        pl.semaphore_signal(barrier, inc=1, device_id={"view": other}, device_id_type=pl.DeviceIdType.MESH)
        return carry

    each_slab(greet)
    greet(partner, 1 - core, 0)
    lax.fori_loop(0, n_view - 1, greet_view, 0)

    loads = []
    for i, (src, dst) in enumerate(
        [
            (ray_hits, hits),
            (fine_axial, axial_f),
            (coarse_axial, axial_c),
            (measured, seen_in),
            (ray_weight, weight_in),
            (margin_blocks, blocks),
            (coarse_volume, vol_c),
            (coarse_weight, wgt_c),
            (fine_volume, vol_in.at[0]),
            (fine_weight, vol_in.at[1]),
        ]
    ):
        copy = pltpu.make_async_copy(src, dst, load_sem.at[i])
        copy.start()
        loads.append(copy)
    ray_loads = []
    for b in range(n_view):
        part = pl.ds(b * width, width)
        pair = []
        for i, (src, dst) in enumerate([(coarse_rays, rays_c), (fine_rays, rays_f)]):
            copy = pltpu.make_async_copy(
                src.at[:, part, :], dst.at[:, part, :], load_sem.at[10 + 2 * b + i]
            )
            copy.start()
            pair.append(copy)
        ray_loads.append(pair)

    for copy in loads[:5]:
        copy.wait()
    half_w = all_w // 2
    row_tile = lax.broadcasted_iota(jnp.int32, (1, all_w), 1) // (all_w // n_tile)
    for v in range(2):
        hit = jnp.zeros((1, all_w), F32)
        for t in range(n_tile):
            hit = jnp.where(row_tile == t, hits[v, 0, t].astype(F32), hit)
        dc = (axial_c[v].astype(F32) * hit).astype(BF16)
        df = axial_f[v].astype(F32) * hit
        df = jnp.concatenate([df[:, :half_w], df[:, half_w:]], axis=0)
        init_send[v, 0] = dc[0:8, :half_w]
        init_send[v, 1] = dc[8:16, :half_w]
        init_send[v, 2] = dc[0:8, half_w:]
        init_send[v, 3] = dc[8:16, half_w:]
        init_send[v, 4] = df.astype(BF16)
        init_send[v, 5] = seen_in[:, v, :].astype(BF16)
        init_send[v, 6] = weight_in[:, v, :].astype(BF16)
    init_all[slab] = init_send[core]

    upper = lax.broadcasted_iota(jnp.int32, (8, 128), 0) >= rows_f

    def fine_half(packed, h):
        mine = upper if h else jnp.logical_not(upper)
        return jnp.where(mine, packed.astype(F32), 0.0).astype(BF16)

    for v in range(2):
        for h in range(2):
            depth = jnp.concatenate(
                [init_send[v, 2 * h], init_send[v, 2 * h + 1], fine_half(init_send[v, 4], h)], axis=0
            )
            depth_own[v, h * half_w : (h + 1) * half_w, :] = depth.T

    def chip_depth(i, index):
        for h in range(2):
            cols = slice(h * half_w, (h + 1) * half_w)
            depth_chip[i, 0:8, cols] = init_all[index, 2 * h]
            depth_chip[i, 8:16, cols] = init_all[index, 2 * h + 1]
            depth_chip[i, 16:24, cols] = fine_half(init_all[index, 4], h)

    chip_depth(0, slab)

    for copy in loads[5:]:
        copy.wait()
    block_id = lax.broadcasted_iota(jnp.int32, (1, cells), 1) // BLOCK
    keep = jnp.ones((1, cells), F32)
    for t in range(margin_blocks.shape[1]):
        keep = jnp.where(block_id == blocks[0, t], 0.0, keep)
    vol_c[...] = vol_c[...] * keep
    wgt_c[...] = wgt_c[...] * keep
    for b in range(n_view):
        for j in range(tiles):
            part = slice(b * width + j * 128, b * width + (j + 1) * 128)
            vol_f[b, j * rows_f : (j + 1) * rows_f, :] = vol_in[0, :, part]
            wgt_f[b, j * rows_f : (j + 1) * rows_f, :] = vol_in[1, :, part]

    group = lax.broadcasted_iota(jnp.int32, (16, 128), 0) // rows_f
    masks = [jnp.where(group == j, 1.0, 0.0).astype(F32) for j in range(tiles)]

    def add_moment(b, acc):
        part = pl.ds(pl.multiple_of(b * width, 128), width)
        lhs_c = vol_c[:, part].astype(BF16)
        packed = vol_f[b]
        lhs_f = jnp.concatenate([(packed * m).astype(BF16) for m in masks], axis=1)
        new = []
        for v in range(2):
            new.append(acc[v] + dot(lhs_c, rays_c[v, part, :]))
        for v in range(2):
            new.append(acc[2 + v] + dot(lhs_f, rays_f[v, part, :]))
        return new

    def finish_moment(k, acc):
        for v in range(2):
            mc = acc[v].astype(BF16)
            half = acc[2 + v][0:8] + acc[2 + v][8:16]
            whole = half + pltpu.roll(half, 4, 0)
            moment_send[k, v, 0] = mc[0:8]
            moment_send[k, v, 1] = mc[8:16]
            moment_send[k, v, 2] = whole.astype(BF16)
        if k > 0:
            moment_all[k, slab] = moment_send[k, core]

    zero = [jnp.zeros((16, 128), F32) for _ in range(4)]
    acc = zero
    for b in range(n_view):
        for copy in ray_loads[b]:
            copy.wait()
        acc = add_moment(b, acc)
    finish_moment(0, acc)
    for v in range(2):
        part = dot(depth_own[v], moment_send[0, v].reshape(24, 128)).astype(BF16)
        for i in range(n_slab):
            part_send[i, v] = part[i * rows_w : (i + 1) * rows_w]
    part_recv[slab] = part_send[slab]

    pl.semaphore_wait(barrier, n_slab + n_view - 2)

    def to_slab(src, dst, send_sem, recv_sem, other):
        return pltpu.make_async_remote_copy(
            src_ref=src,
            dst_ref=dst,
            send_sem=send_sem,
            recv_sem=recv_sem,
            device_id={"slab": other},
            device_id_type=pl.DeviceIdType.MESH,
        )

    def send_init(other, c, dx):
        to_slab(
            init_send.at[c], init_all.at[slab], init_send_sem.at[0], init_recv_sem.at[0], other
        ).start()

    def send_moments(k):
        def send(other, c, dx):
            to_slab(
                moment_send.at[k, c],
                moment_all.at[k, slab],
                moment_send_sem.at[k],
                moment_recv_sem.at[k, 0],
                other,
            ).start()

        each_slab(send)
        send(partner, 1 - core, 0)

    def others(ref, sem_send, sem_recv, count):
        return pltpu.make_async_remote_copy(
            src_ref=ref.at[pl.ds(0, count)],
            dst_ref=ref.at[pl.ds(0, count)],
            send_sem=sem_send,
            recv_sem=sem_recv,
            device_id={"slab": partner},
            device_id_type=pl.DeviceIdType.MESH,
        )

    def send_part(other, c, dx):
        to_slab(
            part_send.at[other],
            part_recv.at[slab],
            first_send_sem.at[0],
            first_recv_sem.at[0],
            other,
        ).start()

    def send_rest(other, c, dx):
        to_slab(
            rest_send.at[c], rest_recv.at[slab], first_send_sem.at[1], first_recv_sem.at[1], other
        ).start()

    each_slab(send_part)
    send_part(partner, 1 - core, 0)
    init_hand = to_slab(
        init_send.at[1 - core], init_all.at[slab], init_send_sem.at[1], init_recv_sem.at[1], partner
    )
    init_hand.start()
    init_hand.wait_recv()
    chip_depth(1, partner)
    others(part_recv, first_send_sem.at[0], first_recv_sem.at[0], n_slab - 1).wait_recv()
    summed = jnp.sum(part_recv[...].astype(F32), axis=0)
    for v in range(2):
        rest_send[v] = (weight_in[:, v, :] * (seen_in[:, v, :] - summed[v])).astype(BF16)
    rest_recv[slab] = rest_send[core]
    each_slab(send_rest)
    send_rest(partner, 1 - core, 0)
    each_slab(send_init, far_chips)

    def finish_init():
        others(init_all, init_send_sem.at[0], init_recv_sem.at[0], n_slab - 2).wait_recv()
        for h in range(2):
            depth = jnp.concatenate(
                [init_all[:, 2 * h], init_all[:, 2 * h + 1], fine_half(init_all[:, 4], h)], axis=1
            )
            depth_t[h * half_w : (h + 1) * half_w, :] = depth.reshape(n_slab * 24, half_w).T
        seen[...] = init_all[:, 5].astype(F32).reshape(n_slab * rows_w, 128)
        weight[...] = init_all[:, 6].astype(F32).reshape(n_slab * rows_w, 128)

    view_order = sorted(
        [(dx, dy) for dx in range(n_xlo) for dy in range(n_y)],
        key=lambda p: -(p[0] + min(p[1], n_y - p[1])),
    )

    def view_of(step):
        dx, dy = step
        return lax.rem(x_lo + dx, n_xlo) * n_y + lax.rem(y + dy, n_y)

    def to_view(src, dst, send_sem, recv_sem, other):
        return pltpu.make_async_remote_copy(
            src_ref=src,
            dst_ref=dst,
            send_sem=send_sem,
            recv_sem=recv_sem,
            device_id={"view": other},
            device_id_type=pl.DeviceIdType.MESH,
        )

    for k in range(ITERS):
        if k == 0:
            others(rest_recv, first_send_sem.at[1], first_recv_sem.at[1], n_slab - 1).wait_recv()
            residual = rest_recv[...].reshape(n_slab * rows_w, 128)
        else:
            send_moments(k)
            if k == 1:
                finish_init()
            others(
                moment_all.at[k], moment_send_sem.at[k], moment_recv_sem.at[k, 0], n_slab - 1
            ).wait_recv()
            projection = dot(depth_t[...], moment_all[k].reshape(n_slab * 24, 128))
            residual = (weight[...] * (seen[...] - projection)).astype(BF16)

        both = dot(depth_chip[...].reshape(48, all_w), residual)

        def spread_of(spread):
            fine = spread[16:24]
            return jnp.concatenate([spread[0:16], fine + pltpu.roll(fine, 4, 0)], axis=0).astype(BF16)

        spread_other = spread_of(both[24:48])
        for i in range(3):
            spread_send[k, i] = spread_other[8 * i : 8 * (i + 1)]
        hand = to_slab(
            spread_send.at[k], spread_recv.at[k], spread_send_sem.at[k], spread_recv_sem.at[k], partner
        )
        hand.start()
        if k == 0:
            each_slab(send_init, near_chips)
        spread_own = spread_of(both[0:24])

        def operands(spread):
            fine = spread[16:24].astype(F32)
            fine = jnp.concatenate([fine, fine], axis=0)
            return spread[0:16], [(fine * m).astype(BF16) for m in masks]

        def terms(coarse, fine, v, b):
            base = b * width
            part = pl.ds(pl.multiple_of(base, 128), width)
            term_c = dot_nt(coarse, rays_c[v, part, :])
            term_f = jnp.zeros((16, 128), F32)
            for j in range(tiles):
                piece = pl.ds(pl.multiple_of(base + j * 128, 128), 128)
                term_f = term_f + dot_nt(fine[j], rays_f[v, piece, :])
            return term_c, term_f

        own_c, own_f = operands(spread_own)
        for i, step in enumerate(view_order):
            term_c, term_f = terms(own_c, own_f, core, view_of(step))
            back_own[i, :, 0:width] = term_c
            back_own[i, :, width : width + 128] = term_f
        hand.wait_recv()
        other_c, other_f = operands(spread_recv[k].reshape(24, 128))
        for i, step in enumerate(view_order):
            b = view_of(step)
            term_c, term_f = terms(other_c, other_f, 1 - core, b)
            term_c = term_c + back_own[i, :, 0:width]
            term_f = term_f + back_own[i, :, width : width + 128]
            dest = back_recv.at[k, view] if step == (0, 0) else back_send.at[k, b]
            for j in range(tiles):
                dest[j] = term_c[:, j * 128 : (j + 1) * 128].astype(BF16)
            dest[tiles] = term_f.astype(BF16)
            if step != (0, 0):
                to_view(
                    back_send.at[k, b],
                    back_recv.at[k, view],
                    back_send_sem.at[k],
                    back_recv_sem.at[k, view],
                    b,
                ).start()
        total = back_recv[k, view].astype(F32)
        for step in reversed(view_order):
            if step == (0, 0):
                continue
            b = view_of(step)
            to_view(
                back_send.at[k, b], back_recv.at[k, b], back_send_sem.at[k], back_recv_sem.at[k, b], b
            ).wait_recv()
            total = total + back_recv[k, b].astype(F32)
        sum_send[k] = total.astype(BF16)
        for step in view_order:
            if step == (0, 0):
                continue
            to_view(
                sum_send.at[k],
                sum_recv.at[k, view],
                sum_send_sem.at[k],
                sum_recv_sem.at[k, view],
                view_of(step),
            ).start()
        acc = zero
        for step in reversed(view_order):
            b = view_of(step)
            if step == (0, 0):
                back = sum_send[k].astype(F32)
            else:
                to_view(
                    sum_send.at[k], sum_recv.at[k, b], sum_send_sem.at[k], sum_recv_sem.at[k, b], b
                ).wait_recv()
                back = sum_recv[k, b].astype(F32)
            for j in range(tiles):
                piece = pl.ds(pl.multiple_of(b * width + j * 128, 128), 128)
                vol_c[:, piece] = vol_c[:, piece] + wgt_c[:, piece] * back[j]
            packed = vol_f[b] + wgt_f[b] * back[tiles]
            if k < ITERS - 1:
                vol_f[b] = packed
                acc = add_moment(b, acc)
            else:
                for j in range(tiles):
                    piece = pl.ds(pl.multiple_of(b * width + j * 128, 128), 128)
                    fine_out[:, piece] = packed[j * rows_f : (j + 1) * rows_f]
        if k < ITERS - 1:
            finish_moment(k + 1, acc)

    others(init_all, init_send_sem.at[0], init_recv_sem.at[0], n_slab - 2).wait_send()
    init_hand.wait_send()
    others(part_recv, first_send_sem.at[0], first_recv_sem.at[0], n_slab - 1).wait_send()
    others(rest_recv, first_send_sem.at[1], first_recv_sem.at[1], n_slab - 1).wait_send()
    for k in range(ITERS):
        if k > 0:
            others(
                moment_all.at[k], moment_send_sem.at[k], moment_recv_sem.at[k, 0], n_slab - 1
            ).wait_send()
        to_slab(
            spread_send.at[k], spread_recv.at[k], spread_send_sem.at[k], spread_recv_sem.at[k], partner
        ).wait_send()
        others(back_send.at[k], back_send_sem.at[k], back_recv_sem.at[k, 0], n_view - 1).wait_send()
        others(back_send.at[k], sum_send_sem.at[k], back_recv_sem.at[k, 0], n_view - 1).wait_send()


def put_out(fine, coarse, fine_out, coarse_out, sem):
    copies = [
        pltpu.make_async_copy(src, dst, sem.at[i])
        for i, (src, dst) in enumerate([(coarse, coarse_out), (fine, fine_out)])
    ]
    for copy in copies:
        copy.start()
    for copy in copies:
        copy.wait()


def build(mesh, n_z, n_y):
    n_slab, n_view = mesh.shape["slab"], mesh.shape["view"]

    def body(*args):
        fine_volume, coarse_volume = args[0], args[1]
        rows_f, cells = fine_volume.shape
        rows_c = coarse_volume.shape[0]
        all_w = args[4].shape[2]
        rows_w = args[6].shape[0]
        width = cells // n_view
        tiles = width // 128
        anyspace = pl.BlockSpec(memory_space=pl.ANY)
        vmem = pl.BlockSpec(memory_space=pltpu.VMEM)
        dma = pltpu.SemaphoreType.DMA
        block = (tiles + 1, 16, 128)
        shapes = ((rows_f, cells), (rows_c, cells))
        results = pl.pallas_call(
            functools.partial(kernel, n_z, n_y, n_slab, n_view),
            name="sirt",
            out_shape=tuple(pltpu.VMEM(shape, F32) for shape in shapes),
            in_specs=[anyspace] * 12,
            out_specs=(vmem, vmem),
            scratch_shapes=[
                pltpu.VMEM((2, cells, 128), BF16),
                pltpu.VMEM((2, cells, 128), BF16),
                pltpu.VMEM(args[4].shape, BF16),
                pltpu.VMEM(args[5].shape, BF16),
                pltpu.VMEM(args[6].shape, F32),
                pltpu.VMEM(args[7].shape, F32),
                pltpu.SMEM(args[10].shape, jnp.int32),
                pltpu.SMEM(args[11].shape, jnp.int32),
                pltpu.VMEM((2, rows_f, cells), F32),
                pltpu.VMEM((n_view, 16, 128), F32),
                pltpu.VMEM((n_view, 16, 128), F32),
                pltpu.VMEM((rows_c, cells), F32),
                pltpu.VMEM((2, 7, 8, 128), BF16),
                pltpu.VMEM((n_slab, 7, 8, 128), BF16),
                pltpu.VMEM((all_w, n_slab * 24), BF16),
                pltpu.VMEM((2, 24, all_w), BF16),
                pltpu.VMEM((2, all_w, 24), BF16),
                pltpu.VMEM((n_slab, 2, rows_w, 128), BF16),
                pltpu.VMEM((n_slab, 2, rows_w, 128), BF16),
                pltpu.VMEM((2, rows_w, 128), BF16),
                pltpu.VMEM((n_slab, rows_w, 128), BF16),
                pltpu.VMEM((n_slab * rows_w, 128), F32),
                pltpu.VMEM((n_slab * rows_w, 128), F32),
                pltpu.VMEM((ITERS, 2, 3, 8, 128), BF16),
                pltpu.VMEM((ITERS, n_slab, 3, 8, 128), BF16),
                pltpu.VMEM((ITERS, 3, 8, 128), BF16),
                pltpu.VMEM((ITERS, 3, 8, 128), BF16),
                pltpu.VMEM((n_view, 16, width + 128), F32),
                pltpu.VMEM((ITERS, n_view) + block, BF16),
                pltpu.VMEM((ITERS, n_view) + block, BF16),
                pltpu.VMEM((ITERS,) + block, BF16),
                pltpu.VMEM((ITERS, n_view) + block, BF16),
                dma((10 + 2 * n_view,)),
                dma((2,)),
                dma((2,)),
                dma((2,)),
                dma((2,)),
                dma((ITERS,)),
                dma((ITERS, 2)),
                dma((ITERS,)),
                dma((ITERS,)),
                dma((ITERS,)),
                dma((ITERS, n_view)),
                dma((ITERS,)),
                dma((ITERS, n_view)),
            ],
            compiler_params=pltpu.CompilerParams(collective_id=0, has_side_effects=True),
        )(*args)
        return pl.pallas_call(
            put_out,
            name="put_out",
            out_shape=tuple(jax.ShapeDtypeStruct(shape, F32) for shape in shapes),
            in_specs=[vmem, vmem],
            out_specs=(anyspace, anyspace),
            scratch_shapes=[dma((2,))],
        )(*(pltpu.with_memory_space_constraint(r, pltpu.VMEM) for r in results))

    return jax.shard_map(
        body,
        mesh=mesh,
        in_specs=(
            P("slab", None),
            P("slab", None),
            P("view", None, None),
            P("view", None, None),
            P("view", "slab", None),
            P("view", "slab", None),
            P("slab", "view", None),
            P("slab", "view", None),
            P("slab", None),
            P("slab", None),
            P("slab", None),
            P("view", "slab", None),
        ),
        out_specs=(P("slab", None), P("slab", None)),
        check_vma=False,
    )


def solution(mesh):
    return build(mesh, 8, 4)
```

```python
import functools

import jax
import jax.numpy as jnp
from jax import lax
from jax.experimental import pallas as pl
from jax.experimental.pallas import tpu as pltpu
from jax.sharding import PartitionSpec as P

ITERS = 3
BLOCK = 128
F32 = jnp.float32
BF16 = jnp.bfloat16


def dot(a, b):
    return lax.dot_general(a, b, (((1,), (0,)), ((), ())), preferred_element_type=F32)


def dot_nt(a, b):
    return lax.dot_general(a, b, (((1,), (1,)), ((), ())), preferred_element_type=F32)


def kernel(
    n_z,
    n_y,
    n_slab,
    n_view,
    fine_volume,
    coarse_volume,
    fine_rays,
    coarse_rays,
    fine_axial,
    coarse_axial,
    measured,
    ray_weight,
    fine_weight,
    coarse_weight,
    margin_blocks,
    ray_hits,
    fine_out,
    coarse_out,
    rays_f,
    rays_c,
    axial_f,
    axial_c,
    seen_in,
    weight_in,
    blocks,
    hits,
    vol_in,
    vol_f,
    wgt_f,
    wgt_c,
    init_send,
    init_all,
    depth_t,
    depth_chip,
    depth_own,
    part_send,
    part_recv,
    rest_send,
    rest_recv,
    seen,
    weight,
    moment_send,
    moment_all,
    spread_send,
    spread_recv,
    back_own,
    back_send,
    back_recv,
    sum_send,
    sum_recv,
    load_sem,
    init_send_sem,
    init_recv_sem,
    first_send_sem,
    first_recv_sem,
    moment_send_sem,
    moment_recv_sem,
    spread_send_sem,
    spread_recv_sem,
    back_send_sem,
    back_recv_sem,
    sum_send_sem,
    sum_recv_sem,
):
    slab = lax.axis_index("slab")
    view = lax.axis_index("view")
    core = lax.rem(slab, 2)
    z = lax.rem(slab // 2, n_z)
    x_hi = slab // (2 * n_z)
    n_xhi = n_slab // (2 * n_z)
    y = lax.rem(view, n_y)
    x_lo = view // n_y
    n_xlo = n_view // n_y
    partner = slab + 1 - 2 * core
    vol_c = coarse_out
    cells = coarse_volume.shape[1]
    width = cells // n_view
    tiles = width // 128
    rows_f = fine_volume.shape[0]
    rows_w = measured.shape[0]
    all_w = fine_axial.shape[2]
    n_tile = ray_hits.shape[2]

    barrier = pltpu.get_barrier_semaphore()

    along_z = sorted(range(n_z), key=lambda dz: -min(dz, n_z - dz))
    far_chips = [(dx, dz) for dx in range(n_xhi - 1, 0, -1) for dz in along_z]
    near_chips = [(0, dz) for dz in along_z if dz]

    def each_slab(send, chips=far_chips + near_chips):
        for dx, dz in chips:
            chip = lax.rem(x_hi + dx, n_xhi) * n_z + lax.rem(z + dz, n_z)
            for c in range(2):
                send(2 * chip + c, c, dx)

    def greet(other, c, dx):
        pl.semaphore_signal(barrier, inc=1, device_id={"slab": other}, device_id_type=pl.DeviceIdType.MESH)

    def greet_view(i, carry):
        other = lax.rem(view + 1 + i, n_view)
        pl.semaphore_signal(barrier, inc=1, device_id={"view": other}, device_id_type=pl.DeviceIdType.MESH)
        return carry

    each_slab(greet)
    greet(partner, 1 - core, 0)
    lax.fori_loop(0, n_view - 1, greet_view, 0)

    loads = []
    for i, (src, dst) in enumerate(
        [
            (ray_hits, hits),
            (fine_axial, axial_f),
            (coarse_axial, axial_c),
            (measured, seen_in),
            (ray_weight, weight_in),
            (margin_blocks, blocks),
            (coarse_volume, vol_c),
            (coarse_weight, wgt_c),
            (fine_volume, vol_in.at[0]),
            (fine_weight, vol_in.at[1]),
        ]
    ):
        copy = pltpu.make_async_copy(src, dst, load_sem.at[i])
        copy.start()
        loads.append(copy)
    ray_loads = []
    for b in range(n_view):
        part = pl.ds(b * width, width)
        pair = []
        for i, (src, dst) in enumerate([(coarse_rays, rays_c), (fine_rays, rays_f)]):
            copy = pltpu.make_async_copy(
                src.at[:, part, :], dst.at[:, part, :], load_sem.at[10 + 2 * b + i]
            )
            copy.start()
            pair.append(copy)
        ray_loads.append(pair)

    for copy in loads[:5]:
        copy.wait()
    half_w = all_w // 2
    row_tile = lax.broadcasted_iota(jnp.int32, (1, all_w), 1) // (all_w // n_tile)
    for v in range(2):
        hit = jnp.zeros((1, all_w), F32)
        for t in range(n_tile):
            hit = jnp.where(row_tile == t, hits[v, 0, t].astype(F32), hit)
        dc = (axial_c[v].astype(F32) * hit).astype(BF16)
        df = axial_f[v].astype(F32) * hit
        df = jnp.concatenate([df[:, :half_w], df[:, half_w:]], axis=0)
        init_send[v, 0] = dc[0:8, :half_w]
        init_send[v, 1] = dc[8:16, :half_w]
        init_send[v, 2] = dc[0:8, half_w:]
        init_send[v, 3] = dc[8:16, half_w:]
        init_send[v, 4] = df.astype(BF16)
        init_send[v, 5] = seen_in[:, v, :].astype(BF16)
        init_send[v, 6] = weight_in[:, v, :].astype(BF16)
    init_all[slab] = init_send[core]

    upper = lax.broadcasted_iota(jnp.int32, (8, 128), 0) >= rows_f

    def fine_half(packed, h):
        mine = upper if h else jnp.logical_not(upper)
        return jnp.where(mine, packed.astype(F32), 0.0).astype(BF16)

    for v in range(2):
        for h in range(2):
            depth = jnp.concatenate(
                [init_send[v, 2 * h], init_send[v, 2 * h + 1], fine_half(init_send[v, 4], h)], axis=0
            )
            depth_own[v, h * half_w : (h + 1) * half_w, :] = depth.T

    def chip_depth(i, index):
        for h in range(2):
            cols = slice(h * half_w, (h + 1) * half_w)
            depth_chip[i, 0:8, cols] = init_all[index, 2 * h]
            depth_chip[i, 8:16, cols] = init_all[index, 2 * h + 1]
            depth_chip[i, 16:24, cols] = fine_half(init_all[index, 4], h)

    chip_depth(0, slab)

    for copy in loads[5:]:
        copy.wait()
    block_id = lax.broadcasted_iota(jnp.int32, (1, cells), 1) // BLOCK
    keep = jnp.ones((1, cells), F32)
    for t in range(margin_blocks.shape[1]):
        keep = jnp.where(block_id == blocks[0, t], 0.0, keep)
    vol_c[...] = vol_c[...] * keep
    wgt_c[...] = wgt_c[...] * keep
    for b in range(n_view):
        for j in range(tiles):
            part = slice(b * width + j * 128, b * width + (j + 1) * 128)
            vol_f[b, j * rows_f : (j + 1) * rows_f, :] = vol_in[0, :, part]
            wgt_f[b, j * rows_f : (j + 1) * rows_f, :] = vol_in[1, :, part]

    group = lax.broadcasted_iota(jnp.int32, (16, 128), 0) // rows_f
    masks = [jnp.where(group == j, 1.0, 0.0).astype(F32) for j in range(tiles)]

    def add_moment(b, acc):
        part = pl.ds(pl.multiple_of(b * width, 128), width)
        lhs_c = vol_c[:, part].astype(BF16)
        packed = vol_f[b]
        lhs_f = jnp.concatenate([(packed * m).astype(BF16) for m in masks], axis=1)
        new = []
        for v in range(2):
            new.append(acc[v] + dot(lhs_c, rays_c[v, part, :]))
        for v in range(2):
            new.append(acc[2 + v] + dot(lhs_f, rays_f[v, part, :]))
        return new

    def finish_moment(k, acc):
        for v in range(2):
            mc = acc[v].astype(BF16)
            half = acc[2 + v][0:8] + acc[2 + v][8:16]
            whole = half + pltpu.roll(half, 4, 0)
            moment_send[k, v, 0] = mc[0:8]
            moment_send[k, v, 1] = mc[8:16]
            moment_send[k, v, 2] = whole.astype(BF16)
        if k > 0:
            moment_all[k, slab] = moment_send[k, core]

    zero = [jnp.zeros((16, 128), F32) for _ in range(4)]
    acc = zero
    for b in range(n_view):
        for copy in ray_loads[b]:
            copy.wait()
        acc = add_moment(b, acc)
    finish_moment(0, acc)
    for v in range(2):
        part = dot(depth_own[v], moment_send[0, v].reshape(24, 128)).astype(BF16)
        for i in range(n_slab):
            part_send[i, v] = part[i * rows_w : (i + 1) * rows_w]
    part_recv[slab] = part_send[slab]

    pl.semaphore_wait(barrier, n_slab + n_view - 2)

    def to_slab(src, dst, send_sem, recv_sem, other):
        return pltpu.make_async_remote_copy(
            src_ref=src,
            dst_ref=dst,
            send_sem=send_sem,
            recv_sem=recv_sem,
            device_id={"slab": other},
            device_id_type=pl.DeviceIdType.MESH,
        )

    def send_init(other, c, dx):
        to_slab(
            init_send.at[c], init_all.at[slab], init_send_sem.at[0], init_recv_sem.at[0], other
        ).start()

    def send_moments(k):
        def send(other, c, dx):
            to_slab(
                moment_send.at[k, c],
                moment_all.at[k, slab],
                moment_send_sem.at[k],
                moment_recv_sem.at[k, 0],
                other,
            ).start()

        each_slab(send)
        send(partner, 1 - core, 0)

    def others(ref, sem_send, sem_recv, count):
        return pltpu.make_async_remote_copy(
            src_ref=ref.at[pl.ds(0, count)],
            dst_ref=ref.at[pl.ds(0, count)],
            send_sem=sem_send,
            recv_sem=sem_recv,
            device_id={"slab": partner},
            device_id_type=pl.DeviceIdType.MESH,
        )

    def send_part(other, c, dx):
        to_slab(
            part_send.at[other],
            part_recv.at[slab],
            first_send_sem.at[0],
            first_recv_sem.at[0],
            other,
        ).start()

    def send_rest(other, c, dx):
        to_slab(
            rest_send.at[c], rest_recv.at[slab], first_send_sem.at[1], first_recv_sem.at[1], other
        ).start()

    each_slab(send_part)
    send_part(partner, 1 - core, 0)
    init_hand = to_slab(
        init_send.at[1 - core], init_all.at[slab], init_send_sem.at[1], init_recv_sem.at[1], partner
    )
    init_hand.start()
    init_hand.wait_recv()
    chip_depth(1, partner)
    others(part_recv, first_send_sem.at[0], first_recv_sem.at[0], n_slab - 1).wait_recv()
    summed = jnp.sum(part_recv[...].astype(F32), axis=0)
    for v in range(2):
        rest_send[v] = (weight_in[:, v, :] * (seen_in[:, v, :] - summed[v])).astype(BF16)
    rest_recv[slab] = rest_send[core]
    each_slab(send_rest)
    send_rest(partner, 1 - core, 0)
    each_slab(send_init, far_chips)

    def finish_init():
        others(init_all, init_send_sem.at[0], init_recv_sem.at[0], n_slab - 2).wait_recv()
        for h in range(2):
            depth = jnp.concatenate(
                [init_all[:, 2 * h], init_all[:, 2 * h + 1], fine_half(init_all[:, 4], h)], axis=1
            )
            depth_t[h * half_w : (h + 1) * half_w, :] = depth.reshape(n_slab * 24, half_w).T
        seen[...] = init_all[:, 5].astype(F32).reshape(n_slab * rows_w, 128)
        weight[...] = init_all[:, 6].astype(F32).reshape(n_slab * rows_w, 128)

    view_order = sorted(
        [(dx, dy) for dx in range(n_xlo) for dy in range(n_y)],
        key=lambda p: -(p[0] + min(p[1], n_y - p[1])),
    )

    hops = [lambda p, h=h: p[0] + min(p[1], n_y - p[1]) == h for h in range(n_y // 2 + n_xlo)]
    groups = [[p for p in view_order if same(p)] for same in hops]

    def view_of(step):
        dx, dy = step
        return lax.rem(x_lo + dx, n_xlo) * n_y + lax.rem(y + dy, n_y)

    def to_view(src, dst, send_sem, recv_sem, other):
        return pltpu.make_async_remote_copy(
            src_ref=src,
            dst_ref=dst,
            send_sem=send_sem,
            recv_sem=recv_sem,
            device_id={"view": other},
            device_id_type=pl.DeviceIdType.MESH,
        )

    for k in range(ITERS):
        if k == 0:
            others(rest_recv, first_send_sem.at[1], first_recv_sem.at[1], n_slab - 1).wait_recv()
            residual = rest_recv[...].reshape(n_slab * rows_w, 128)
        else:
            send_moments(k)
            if k == 1:
                finish_init()
            others(
                moment_all.at[k], moment_send_sem.at[k], moment_recv_sem.at[k, 0], n_slab - 1
            ).wait_recv()
            projection = dot(depth_t[...], moment_all[k].reshape(n_slab * 24, 128))
            residual = (weight[...] * (seen[...] - projection)).astype(BF16)

        both = dot(depth_chip[...].reshape(48, all_w), residual)

        def spread_of(spread):
            fine = spread[16:24]
            return jnp.concatenate([spread[0:16], fine + pltpu.roll(fine, 4, 0)], axis=0).astype(BF16)

        spread_other = spread_of(both[24:48])
        for i in range(3):
            spread_send[k, i] = spread_other[8 * i : 8 * (i + 1)]
        hand = to_slab(
            spread_send.at[k], spread_recv.at[k], spread_send_sem.at[k], spread_recv_sem.at[k], partner
        )
        hand.start()
        if k == 0:
            each_slab(send_init, near_chips)
        spread_own = spread_of(both[0:24])

        def operands(spread):
            fine = spread[16:24].astype(F32)
            fine = jnp.concatenate([fine, fine], axis=0)
            return spread[0:16], [(fine * m).astype(BF16) for m in masks]

        def terms(coarse, fine, v, b):
            base = b * width
            part = pl.ds(pl.multiple_of(base, 128), width)
            term_c = dot_nt(coarse, rays_c[v, part, :])
            term_f = jnp.zeros((16, 128), F32)
            for j in range(tiles):
                piece = pl.ds(pl.multiple_of(base + j * 128, 128), 128)
                term_f = term_f + dot_nt(fine[j], rays_f[v, piece, :])
            return term_c, term_f

        own_c, own_f = operands(spread_own)
        for i, step in enumerate(view_order):
            term_c, term_f = terms(own_c, own_f, core, view_of(step))
            back_own[i, :, 0:width] = term_c
            back_own[i, :, width : width + 128] = term_f
        hand.wait_recv()
        other_c, other_f = operands(spread_recv[k].reshape(24, 128))
        def hand_out(step, term_c, term_f):
            b = view_of(step)
            dest = back_recv.at[k, view] if step == (0, 0) else back_send.at[k, b]
            for j in range(tiles):
                dest[j] = term_c[:, j * 128 : (j + 1) * 128].astype(BF16)
            dest[tiles] = term_f.astype(BF16)
            if step != (0, 0):
                to_view(
                    back_send.at[k, b],
                    back_recv.at[k, view],
                    back_send_sem.at[k],
                    back_recv_sem.at[k, view],
                    b,
                ).start()

        ready = None
        for i, step in enumerate(view_order):
            term_c, term_f = terms(other_c, other_f, 1 - core, view_of(step))
            if ready is not None:
                hand_out(*ready)
            term_c = term_c + back_own[i, :, 0:width]
            term_f = term_f + back_own[i, :, width : width + 128]
            ready = (step, term_c, term_f)
        hand_out(*ready)
        total = back_recv[k, view].astype(F32)
        for step in reversed(view_order):
            if step == (0, 0):
                continue
            b = view_of(step)
            to_view(
                back_send.at[k, b], back_recv.at[k, b], back_send_sem.at[k], back_recv_sem.at[k, b], b
            ).wait_recv()
            total = total + back_recv[k, b].astype(F32)
        sum_send[k] = total.astype(BF16)
        for step in view_order:
            if step == (0, 0):
                continue
            to_view(
                sum_send.at[k],
                sum_recv.at[k, view],
                sum_send_sem.at[k],
                sum_recv_sem.at[k, view],
                view_of(step),
            ).start()
        acc = zero
        for group in groups:
            for step in group:
                if step != (0, 0):
                    b = view_of(step)
                    to_view(
                        sum_send.at[k], sum_recv.at[k, b], sum_send_sem.at[k], sum_recv_sem.at[k, b], b
                    ).wait_recv()
            for step in group:
                b = view_of(step)
                back = (sum_send[k] if step == (0, 0) else sum_recv[k, b]).astype(F32)
                for j in range(tiles):
                    piece = pl.ds(pl.multiple_of(b * width + j * 128, 128), 128)
                    vol_c[:, piece] = vol_c[:, piece] + wgt_c[:, piece] * back[j]
                packed = vol_f[b] + wgt_f[b] * back[tiles]
                if k < ITERS - 1:
                    vol_f[b] = packed
                    acc = add_moment(b, acc)
                else:
                    for j in range(tiles):
                        piece = pl.ds(pl.multiple_of(b * width + j * 128, 128), 128)
                        fine_out[:, piece] = packed[j * rows_f : (j + 1) * rows_f]
        if k < ITERS - 1:
            finish_moment(k + 1, acc)

    others(init_all, init_send_sem.at[0], init_recv_sem.at[0], n_slab - 2).wait_send()
    init_hand.wait_send()
    others(part_recv, first_send_sem.at[0], first_recv_sem.at[0], n_slab - 1).wait_send()
    others(rest_recv, first_send_sem.at[1], first_recv_sem.at[1], n_slab - 1).wait_send()
    for k in range(ITERS):
        if k > 0:
            others(
                moment_all.at[k], moment_send_sem.at[k], moment_recv_sem.at[k, 0], n_slab - 1
            ).wait_send()
        to_slab(
            spread_send.at[k], spread_recv.at[k], spread_send_sem.at[k], spread_recv_sem.at[k], partner
        ).wait_send()
        others(back_send.at[k], back_send_sem.at[k], back_recv_sem.at[k, 0], n_view - 1).wait_send()
        others(back_send.at[k], sum_send_sem.at[k], back_recv_sem.at[k, 0], n_view - 1).wait_send()


def put_out(fine, coarse, fine_out, coarse_out, sem):
    copies = [
        pltpu.make_async_copy(src, dst, sem.at[i])
        for i, (src, dst) in enumerate([(coarse, coarse_out), (fine, fine_out)])
    ]
    for copy in copies:
        copy.start()
    for copy in copies:
        copy.wait()


def build(mesh, n_z, n_y):
    n_slab, n_view = mesh.shape["slab"], mesh.shape["view"]

    def body(*args):
        fine_volume, coarse_volume = args[0], args[1]
        rows_f, cells = fine_volume.shape
        rows_c = coarse_volume.shape[0]
        all_w = args[4].shape[2]
        rows_w = args[6].shape[0]
        width = cells // n_view
        tiles = width // 128
        anyspace = pl.BlockSpec(memory_space=pl.ANY)
        vmem = pl.BlockSpec(memory_space=pltpu.VMEM)
        dma = pltpu.SemaphoreType.DMA
        block = (tiles + 1, 16, 128)
        shapes = ((rows_f, cells), (rows_c, cells))
        results = pl.pallas_call(
            functools.partial(kernel, n_z, n_y, n_slab, n_view),
            name="sirt",
            out_shape=tuple(pltpu.VMEM(shape, F32) for shape in shapes),
            in_specs=[anyspace] * 12,
            out_specs=(vmem, vmem),
            scratch_shapes=[
                pltpu.VMEM((2, cells, 128), BF16),
                pltpu.VMEM((2, cells, 128), BF16),
                pltpu.VMEM(args[4].shape, BF16),
                pltpu.VMEM(args[5].shape, BF16),
                pltpu.VMEM(args[6].shape, F32),
                pltpu.VMEM(args[7].shape, F32),
                pltpu.SMEM(args[10].shape, jnp.int32),
                pltpu.SMEM(args[11].shape, jnp.int32),
                pltpu.VMEM((2, rows_f, cells), F32),
                pltpu.VMEM((n_view, 16, 128), F32),
                pltpu.VMEM((n_view, 16, 128), F32),
                pltpu.VMEM((rows_c, cells), F32),
                pltpu.VMEM((2, 7, 8, 128), BF16),
                pltpu.VMEM((n_slab, 7, 8, 128), BF16),
                pltpu.VMEM((all_w, n_slab * 24), BF16),
                pltpu.VMEM((2, 24, all_w), BF16),
                pltpu.VMEM((2, all_w, 24), BF16),
                pltpu.VMEM((n_slab, 2, rows_w, 128), BF16),
                pltpu.VMEM((n_slab, 2, rows_w, 128), BF16),
                pltpu.VMEM((2, rows_w, 128), BF16),
                pltpu.VMEM((n_slab, rows_w, 128), BF16),
                pltpu.VMEM((n_slab * rows_w, 128), F32),
                pltpu.VMEM((n_slab * rows_w, 128), F32),
                pltpu.VMEM((ITERS, 2, 3, 8, 128), BF16),
                pltpu.VMEM((ITERS, n_slab, 3, 8, 128), BF16),
                pltpu.VMEM((ITERS, 3, 8, 128), BF16),
                pltpu.VMEM((ITERS, 3, 8, 128), BF16),
                pltpu.VMEM((n_view, 16, width + 128), F32),
                pltpu.VMEM((ITERS, n_view) + block, BF16),
                pltpu.VMEM((ITERS, n_view) + block, BF16),
                pltpu.VMEM((ITERS,) + block, BF16),
                pltpu.VMEM((ITERS, n_view) + block, BF16),
                dma((10 + 2 * n_view,)),
                dma((2,)),
                dma((2,)),
                dma((2,)),
                dma((2,)),
                dma((ITERS,)),
                dma((ITERS, 2)),
                dma((ITERS,)),
                dma((ITERS,)),
                dma((ITERS,)),
                dma((ITERS, n_view)),
                dma((ITERS,)),
                dma((ITERS, n_view)),
            ],
            compiler_params=pltpu.CompilerParams(collective_id=0, has_side_effects=True),
        )(*args)
        return pl.pallas_call(
            put_out,
            name="put_out",
            out_shape=tuple(jax.ShapeDtypeStruct(shape, F32) for shape in shapes),
            in_specs=[vmem, vmem],
            out_specs=(anyspace, anyspace),
            scratch_shapes=[dma((2,))],
        )(*(pltpu.with_memory_space_constraint(r, pltpu.VMEM) for r in results))

    return jax.shard_map(
        body,
        mesh=mesh,
        in_specs=(
            P("slab", None),
            P("slab", None),
            P("view", None, None),
            P("view", None, None),
            P("view", "slab", None),
            P("view", "slab", None),
            P("slab", "view", None),
            P("slab", "view", None),
            P("slab", None),
            P("slab", None),
            P("slab", None),
            P("view", "slab", None),
        ),
        out_specs=(P("slab", None), P("slab", None)),
        check_vma=False,
    )


def solution(mesh):
    return build(mesh, 8, 4)
```

```python
import functools

import jax
import jax.numpy as jnp
from jax import lax
from jax.experimental import pallas as pl
from jax.experimental.pallas import tpu as pltpu
from jax.sharding import PartitionSpec as P

ITERS = 3
BLOCK = 128
F32 = jnp.float32
BF16 = jnp.bfloat16


def dot(a, b):
    return lax.dot_general(a, b, (((1,), (0,)), ((), ())), preferred_element_type=F32)


def dot_nt(a, b):
    return lax.dot_general(a, b, (((1,), (1,)), ((), ())), preferred_element_type=F32)


def kernel(
    n_z,
    n_y,
    n_slab,
    n_view,
    fine_volume,
    coarse_volume,
    fine_rays,
    coarse_rays,
    fine_axial,
    coarse_axial,
    measured,
    ray_weight,
    fine_weight,
    coarse_weight,
    margin_blocks,
    ray_hits,
    fine_out,
    coarse_out,
    rays_f,
    rays_c,
    axial_f,
    axial_c,
    seen_in,
    weight_in,
    blocks,
    hits,
    vol_in,
    vol_f,
    wgt_f,
    wgt_c,
    init_send,
    init_all,
    depth_t,
    depth_chip,
    depth_own,
    part_send,
    part_recv,
    rest_send,
    rest_recv,
    seen,
    weight,
    moment_send,
    moment_all,
    spread_send,
    spread_recv,
    back_own,
    back_send,
    back_recv,
    sum_send,
    sum_recv,
    load_sem,
    init_send_sem,
    init_recv_sem,
    first_send_sem,
    first_recv_sem,
    moment_send_sem,
    moment_recv_sem,
    spread_send_sem,
    spread_recv_sem,
    back_send_sem,
    back_recv_sem,
    sum_send_sem,
    sum_recv_sem,
):
    slab = lax.axis_index("slab")
    view = lax.axis_index("view")
    core = lax.rem(slab, 2)
    z = lax.rem(slab // 2, n_z)
    x_hi = slab // (2 * n_z)
    n_xhi = n_slab // (2 * n_z)
    y = lax.rem(view, n_y)
    x_lo = view // n_y
    n_xlo = n_view // n_y
    partner = slab + 1 - 2 * core
    vol_c = coarse_out
    cells = coarse_volume.shape[1]
    width = cells // n_view
    tiles = width // 128
    rows_f = fine_volume.shape[0]
    rows_w = measured.shape[0]
    all_w = fine_axial.shape[2]
    n_tile = ray_hits.shape[2]

    barrier = pltpu.get_barrier_semaphore()

    along_z = sorted(range(n_z), key=lambda dz: -min(dz, n_z - dz))
    far_chips = [(dx, dz) for dx in range(n_xhi - 1, 0, -1) for dz in along_z]
    near_chips = [(0, dz) for dz in along_z if dz]

    def each_slab(send, chips=far_chips + near_chips):
        for dx, dz in chips:
            chip = lax.rem(x_hi + dx, n_xhi) * n_z + lax.rem(z + dz, n_z)
            for c in range(2):
                send(2 * chip + c, c, dx)

    def greet(other, c, dx):
        pl.semaphore_signal(barrier, inc=1, device_id={"slab": other}, device_id_type=pl.DeviceIdType.MESH)

    def greet_view(i, carry):
        other = lax.rem(view + 1 + i, n_view)
        pl.semaphore_signal(barrier, inc=1, device_id={"view": other}, device_id_type=pl.DeviceIdType.MESH)
        return carry

    each_slab(greet)
    greet(partner, 1 - core, 0)
    lax.fori_loop(0, n_view - 1, greet_view, 0)

    loads = []
    for i, (src, dst) in enumerate(
        [
            (ray_hits, hits),
            (fine_axial, axial_f),
            (coarse_axial, axial_c),
            (measured, seen_in),
            (ray_weight, weight_in),
            (margin_blocks, blocks),
            (coarse_volume, vol_c),
            (coarse_weight, wgt_c),
            (fine_volume, vol_in.at[0]),
            (fine_weight, vol_in.at[1]),
        ]
    ):
        copy = pltpu.make_async_copy(src, dst, load_sem.at[i])
        copy.start()
        loads.append(copy)
    ray_loads = []
    for b in range(n_view):
        part = pl.ds(b * width, width)
        pair = []
        for i, (src, dst) in enumerate([(coarse_rays, rays_c), (fine_rays, rays_f)]):
            copy = pltpu.make_async_copy(
                src.at[:, part, :], dst.at[:, part, :], load_sem.at[10 + 2 * b + i]
            )
            copy.start()
            pair.append(copy)
        ray_loads.append(pair)

    for copy in loads[:5]:
        copy.wait()
    half_w = all_w // 2
    row_tile = lax.broadcasted_iota(jnp.int32, (1, all_w), 1) // (all_w // n_tile)
    for v in range(2):
        hit = jnp.zeros((1, all_w), F32)
        for t in range(n_tile):
            hit = jnp.where(row_tile == t, hits[v, 0, t].astype(F32), hit)
        dc = (axial_c[v].astype(F32) * hit).astype(BF16)
        df = axial_f[v].astype(F32) * hit
        df = jnp.concatenate([df[:, :half_w], df[:, half_w:]], axis=0)
        init_send[v, 0] = dc[0:8, :half_w]
        init_send[v, 1] = dc[8:16, :half_w]
        init_send[v, 2] = dc[0:8, half_w:]
        init_send[v, 3] = dc[8:16, half_w:]
        init_send[v, 4] = df.astype(BF16)
        init_send[v, 5] = seen_in[:, v, :].astype(BF16)
        init_send[v, 6] = weight_in[:, v, :].astype(BF16)
    init_all[slab] = init_send[core]

    upper = lax.broadcasted_iota(jnp.int32, (8, 128), 0) >= rows_f

    def fine_half(packed, h):
        mine = upper if h else jnp.logical_not(upper)
        return jnp.where(mine, packed.astype(F32), 0.0).astype(BF16)

    for v in range(2):
        for h in range(2):
            depth = jnp.concatenate(
                [init_send[v, 2 * h], init_send[v, 2 * h + 1], fine_half(init_send[v, 4], h)], axis=0
            )
            depth_own[v, h * half_w : (h + 1) * half_w, :] = depth.T

    def chip_depth(i, index):
        for h in range(2):
            cols = slice(h * half_w, (h + 1) * half_w)
            depth_chip[i, 0:8, cols] = init_all[index, 2 * h]
            depth_chip[i, 8:16, cols] = init_all[index, 2 * h + 1]
            depth_chip[i, 16:24, cols] = fine_half(init_all[index, 4], h)

    chip_depth(0, slab)

    for copy in loads[5:]:
        copy.wait()
    block_id = lax.broadcasted_iota(jnp.int32, (1, cells), 1) // BLOCK
    keep = jnp.ones((1, cells), F32)
    for t in range(margin_blocks.shape[1]):
        keep = jnp.where(block_id == blocks[0, t], 0.0, keep)
    vol_c[...] = vol_c[...] * keep
    wgt_c[...] = wgt_c[...] * keep
    for b in range(n_view):
        for j in range(tiles):
            part = slice(b * width + j * 128, b * width + (j + 1) * 128)
            vol_f[b, j * rows_f : (j + 1) * rows_f, :] = vol_in[0, :, part]
            wgt_f[b, j * rows_f : (j + 1) * rows_f, :] = vol_in[1, :, part]

    group = lax.broadcasted_iota(jnp.int32, (16, 128), 0) // rows_f
    masks = [jnp.where(group == j, 1.0, 0.0).astype(F32) for j in range(tiles)]

    def add_moment(b, acc):
        part = pl.ds(pl.multiple_of(b * width, 128), width)
        lhs_c = vol_c[:, part].astype(BF16)
        packed = vol_f[b]
        lhs_f = jnp.concatenate([(packed * m).astype(BF16) for m in masks], axis=1)
        new = []
        for v in range(2):
            new.append(acc[v] + dot(lhs_c, rays_c[v, part, :]))
        for v in range(2):
            new.append(acc[2 + v] + dot(lhs_f, rays_f[v, part, :]))
        return new

    def finish_moment(k, acc):
        for v in range(2):
            mc = acc[v].astype(BF16)
            half = acc[2 + v][0:8] + acc[2 + v][8:16]
            whole = half + pltpu.roll(half, 4, 0)
            moment_send[k, v, 0] = mc[0:8]
            moment_send[k, v, 1] = mc[8:16]
            moment_send[k, v, 2] = whole.astype(BF16)
        if k > 0:
            moment_all[k, slab] = moment_send[k, core]

    zero = [jnp.zeros((16, 128), F32) for _ in range(4)]
    acc = zero
    for b in range(n_view):
        for copy in ray_loads[b]:
            copy.wait()
        acc = add_moment(b, acc)
    finish_moment(0, acc)
    for v in range(2):
        part = dot(depth_own[v], moment_send[0, v].reshape(24, 128)).astype(BF16)
        for i in range(n_slab):
            part_send[i, v] = part[i * rows_w : (i + 1) * rows_w]
    part_recv[slab] = part_send[slab]

    pl.semaphore_wait(barrier, n_slab + n_view - 2)

    def to_slab(src, dst, send_sem, recv_sem, other):
        return pltpu.make_async_remote_copy(
            src_ref=src,
            dst_ref=dst,
            send_sem=send_sem,
            recv_sem=recv_sem,
            device_id={"slab": other},
            device_id_type=pl.DeviceIdType.MESH,
        )

    def send_init(other, c, dx):
        to_slab(
            init_send.at[c], init_all.at[slab], init_send_sem.at[0], init_recv_sem.at[0], other
        ).start()

    def send_moments(k):
        def send(other, c, dx):
            to_slab(
                moment_send.at[k, c],
                moment_all.at[k, slab],
                moment_send_sem.at[k],
                moment_recv_sem.at[k, 0],
                other,
            ).start()

        each_slab(send)
        send(partner, 1 - core, 0)

    def others(ref, sem_send, sem_recv, count):
        return pltpu.make_async_remote_copy(
            src_ref=ref.at[pl.ds(0, count)],
            dst_ref=ref.at[pl.ds(0, count)],
            send_sem=sem_send,
            recv_sem=sem_recv,
            device_id={"slab": partner},
            device_id_type=pl.DeviceIdType.MESH,
        )

    def send_part(other, c, dx):
        to_slab(
            part_send.at[other],
            part_recv.at[slab],
            first_send_sem.at[0],
            first_recv_sem.at[0],
            other,
        ).start()

    def send_rest(other, c, dx):
        to_slab(
            rest_send.at[c], rest_recv.at[slab], first_send_sem.at[1], first_recv_sem.at[1], other
        ).start()

    each_slab(send_part)
    send_part(partner, 1 - core, 0)
    init_hand = to_slab(
        init_send.at[1 - core], init_all.at[slab], init_send_sem.at[1], init_recv_sem.at[1], partner
    )
    init_hand.start()
    init_hand.wait_recv()
    chip_depth(1, partner)
    others(part_recv, first_send_sem.at[0], first_recv_sem.at[0], n_slab - 1).wait_recv()
    summed = jnp.sum(part_recv[...].astype(F32), axis=0)
    for v in range(2):
        rest_send[v] = (weight_in[:, v, :] * (seen_in[:, v, :] - summed[v])).astype(BF16)
    rest_recv[slab] = rest_send[core]
    each_slab(send_rest)
    send_rest(partner, 1 - core, 0)
    each_slab(send_init, far_chips)

    def finish_init():
        others(init_all, init_send_sem.at[0], init_recv_sem.at[0], n_slab - 2).wait_recv()
        for h in range(2):
            depth = jnp.concatenate(
                [init_all[:, 2 * h], init_all[:, 2 * h + 1], fine_half(init_all[:, 4], h)], axis=1
            )
            depth_t[h * half_w : (h + 1) * half_w, :] = depth.reshape(n_slab * 24, half_w).T
        seen[...] = init_all[:, 5].astype(F32).reshape(n_slab * rows_w, 128)
        weight[...] = init_all[:, 6].astype(F32).reshape(n_slab * rows_w, 128)

    view_order = sorted(
        [(dx, dy) for dx in range(n_xlo) for dy in range(n_y)],
        key=lambda p: -(p[0] + min(p[1], n_y - p[1])),
    )

    hops = [lambda p, h=h: p[0] + min(p[1], n_y - p[1]) == h for h in range(n_y // 2 + n_xlo)]
    groups = [[p for p in view_order if same(p)] for same in hops]

    def view_of(step):
        dx, dy = step
        return lax.rem(x_lo + dx, n_xlo) * n_y + lax.rem(y + dy, n_y)

    def to_view(src, dst, send_sem, recv_sem, other):
        return pltpu.make_async_remote_copy(
            src_ref=src,
            dst_ref=dst,
            send_sem=send_sem,
            recv_sem=recv_sem,
            device_id={"view": other},
            device_id_type=pl.DeviceIdType.MESH,
        )

    for k in range(ITERS):
        if k == 0:
            others(rest_recv, first_send_sem.at[1], first_recv_sem.at[1], n_slab - 1).wait_recv()
            residual = rest_recv[...].reshape(n_slab * rows_w, 128)
        else:
            send_moments(k)
            if k == 1:
                finish_init()
            others(
                moment_all.at[k], moment_send_sem.at[k], moment_recv_sem.at[k, 0], n_slab - 1
            ).wait_recv()
            projection = dot(depth_t[...], moment_all[k].reshape(n_slab * 24, 128))
            residual = (weight[...] * (seen[...] - projection)).astype(BF16)

        both = dot(depth_chip[...].reshape(48, all_w), residual)

        def spread_of(spread):
            fine = spread[16:24]
            return jnp.concatenate([spread[0:16], fine + pltpu.roll(fine, 4, 0)], axis=0).astype(BF16)

        spread_other = spread_of(both[24:48])
        for i in range(3):
            spread_send[k, i] = spread_other[8 * i : 8 * (i + 1)]
        hand = to_slab(
            spread_send.at[k], spread_recv.at[k], spread_send_sem.at[k], spread_recv_sem.at[k], partner
        )
        hand.start()
        spread_own = spread_of(both[0:24])

        def operands(spread):
            fine = spread[16:24].astype(F32)
            fine = jnp.concatenate([fine, fine], axis=0)
            return spread[0:16], [(fine * m).astype(BF16) for m in masks]

        def terms(coarse, fine, v, b):
            base = b * width
            part = pl.ds(pl.multiple_of(base, 128), width)
            term_c = dot_nt(coarse, rays_c[v, part, :])
            term_f = jnp.zeros((16, 128), F32)
            for j in range(tiles):
                piece = pl.ds(pl.multiple_of(base + j * 128, 128), 128)
                term_f = term_f + dot_nt(fine[j], rays_f[v, piece, :])
            return term_c, term_f

        own_c, own_f = operands(spread_own)
        for i, step in enumerate(view_order):
            term_c, term_f = terms(own_c, own_f, core, view_of(step))
            back_own[i, :, 0:width] = term_c
            back_own[i, :, width : width + 128] = term_f
        hand.wait_recv()
        other_c, other_f = operands(spread_recv[k].reshape(24, 128))
        def hand_out(step, term_c, term_f):
            b = view_of(step)
            dest = back_recv.at[k, view] if step == (0, 0) else back_send.at[k, b]
            for j in range(tiles):
                dest[j] = term_c[:, j * 128 : (j + 1) * 128].astype(BF16)
            dest[tiles] = term_f.astype(BF16)
            if step != (0, 0):
                to_view(
                    back_send.at[k, b],
                    back_recv.at[k, view],
                    back_send_sem.at[k],
                    back_recv_sem.at[k, view],
                    b,
                ).start()

        ready = None
        for i, step in enumerate(view_order):
            term_c, term_f = terms(other_c, other_f, 1 - core, view_of(step))
            if ready is not None:
                hand_out(*ready)
            term_c = term_c + back_own[i, :, 0:width]
            term_f = term_f + back_own[i, :, width : width + 128]
            ready = (step, term_c, term_f)
        hand_out(*ready)
        if k == 0:
            each_slab(send_init, near_chips)
        total = back_recv[k, view].astype(F32)
        for step in reversed(view_order):
            if step == (0, 0):
                continue
            b = view_of(step)
            to_view(
                back_send.at[k, b], back_recv.at[k, b], back_send_sem.at[k], back_recv_sem.at[k, b], b
            ).wait_recv()
            total = total + back_recv[k, b].astype(F32)
        sum_send[k] = total.astype(BF16)
        for step in view_order:
            if step == (0, 0):
                continue
            to_view(
                sum_send.at[k],
                sum_recv.at[k, view],
                sum_send_sem.at[k],
                sum_recv_sem.at[k, view],
                view_of(step),
            ).start()
        acc = zero
        for group in groups:
            for step in group:
                if step != (0, 0):
                    b = view_of(step)
                    to_view(
                        sum_send.at[k], sum_recv.at[k, b], sum_send_sem.at[k], sum_recv_sem.at[k, b], b
                    ).wait_recv()
            for step in group:
                b = view_of(step)
                back = (sum_send[k] if step == (0, 0) else sum_recv[k, b]).astype(F32)
                for j in range(tiles):
                    piece = pl.ds(pl.multiple_of(b * width + j * 128, 128), 128)
                    vol_c[:, piece] = vol_c[:, piece] + wgt_c[:, piece] * back[j]
                packed = vol_f[b] + wgt_f[b] * back[tiles]
                if k < ITERS - 1:
                    vol_f[b] = packed
                    acc = add_moment(b, acc)
                else:
                    for j in range(tiles):
                        piece = pl.ds(pl.multiple_of(b * width + j * 128, 128), 128)
                        fine_out[:, piece] = packed[j * rows_f : (j + 1) * rows_f]
        if k < ITERS - 1:
            finish_moment(k + 1, acc)

    others(init_all, init_send_sem.at[0], init_recv_sem.at[0], n_slab - 2).wait_send()
    init_hand.wait_send()
    others(part_recv, first_send_sem.at[0], first_recv_sem.at[0], n_slab - 1).wait_send()
    others(rest_recv, first_send_sem.at[1], first_recv_sem.at[1], n_slab - 1).wait_send()
    for k in range(ITERS):
        if k > 0:
            others(
                moment_all.at[k], moment_send_sem.at[k], moment_recv_sem.at[k, 0], n_slab - 1
            ).wait_send()
        to_slab(
            spread_send.at[k], spread_recv.at[k], spread_send_sem.at[k], spread_recv_sem.at[k], partner
        ).wait_send()
        others(back_send.at[k], back_send_sem.at[k], back_recv_sem.at[k, 0], n_view - 1).wait_send()
        others(back_send.at[k], sum_send_sem.at[k], back_recv_sem.at[k, 0], n_view - 1).wait_send()


def put_out(fine, coarse, fine_out, coarse_out, sem):
    copies = [
        pltpu.make_async_copy(src, dst, sem.at[i])
        for i, (src, dst) in enumerate([(coarse, coarse_out), (fine, fine_out)])
    ]
    for copy in copies:
        copy.start()
    for copy in copies:
        copy.wait()


def build(mesh, n_z, n_y):
    n_slab, n_view = mesh.shape["slab"], mesh.shape["view"]

    def body(*args):
        fine_volume, coarse_volume = args[0], args[1]
        rows_f, cells = fine_volume.shape
        rows_c = coarse_volume.shape[0]
        all_w = args[4].shape[2]
        rows_w = args[6].shape[0]
        width = cells // n_view
        tiles = width // 128
        anyspace = pl.BlockSpec(memory_space=pl.ANY)
        vmem = pl.BlockSpec(memory_space=pltpu.VMEM)
        dma = pltpu.SemaphoreType.DMA
        block = (tiles + 1, 16, 128)
        shapes = ((rows_f, cells), (rows_c, cells))
        results = pl.pallas_call(
            functools.partial(kernel, n_z, n_y, n_slab, n_view),
            name="sirt",
            out_shape=tuple(pltpu.VMEM(shape, F32) for shape in shapes),
            in_specs=[anyspace] * 12,
            out_specs=(vmem, vmem),
            scratch_shapes=[
                pltpu.VMEM((2, cells, 128), BF16),
                pltpu.VMEM((2, cells, 128), BF16),
                pltpu.VMEM(args[4].shape, BF16),
                pltpu.VMEM(args[5].shape, BF16),
                pltpu.VMEM(args[6].shape, F32),
                pltpu.VMEM(args[7].shape, F32),
                pltpu.SMEM(args[10].shape, jnp.int32),
                pltpu.SMEM(args[11].shape, jnp.int32),
                pltpu.VMEM((2, rows_f, cells), F32),
                pltpu.VMEM((n_view, 16, 128), F32),
                pltpu.VMEM((n_view, 16, 128), F32),
                pltpu.VMEM((rows_c, cells), F32),
                pltpu.VMEM((2, 7, 8, 128), BF16),
                pltpu.VMEM((n_slab, 7, 8, 128), BF16),
                pltpu.VMEM((all_w, n_slab * 24), BF16),
                pltpu.VMEM((2, 24, all_w), BF16),
                pltpu.VMEM((2, all_w, 24), BF16),
                pltpu.VMEM((n_slab, 2, rows_w, 128), BF16),
                pltpu.VMEM((n_slab, 2, rows_w, 128), BF16),
                pltpu.VMEM((2, rows_w, 128), BF16),
                pltpu.VMEM((n_slab, rows_w, 128), BF16),
                pltpu.VMEM((n_slab * rows_w, 128), F32),
                pltpu.VMEM((n_slab * rows_w, 128), F32),
                pltpu.VMEM((ITERS, 2, 3, 8, 128), BF16),
                pltpu.VMEM((ITERS, n_slab, 3, 8, 128), BF16),
                pltpu.VMEM((ITERS, 3, 8, 128), BF16),
                pltpu.VMEM((ITERS, 3, 8, 128), BF16),
                pltpu.VMEM((n_view, 16, width + 128), F32),
                pltpu.VMEM((ITERS, n_view) + block, BF16),
                pltpu.VMEM((ITERS, n_view) + block, BF16),
                pltpu.VMEM((ITERS,) + block, BF16),
                pltpu.VMEM((ITERS, n_view) + block, BF16),
                dma((10 + 2 * n_view,)),
                dma((2,)),
                dma((2,)),
                dma((2,)),
                dma((2,)),
                dma((ITERS,)),
                dma((ITERS, 2)),
                dma((ITERS,)),
                dma((ITERS,)),
                dma((ITERS,)),
                dma((ITERS, n_view)),
                dma((ITERS,)),
                dma((ITERS, n_view)),
            ],
            compiler_params=pltpu.CompilerParams(collective_id=0, has_side_effects=True),
        )(*args)
        return pl.pallas_call(
            put_out,
            name="put_out",
            out_shape=tuple(jax.ShapeDtypeStruct(shape, F32) for shape in shapes),
            in_specs=[vmem, vmem],
            out_specs=(anyspace, anyspace),
            scratch_shapes=[dma((2,))],
        )(*(pltpu.with_memory_space_constraint(r, pltpu.VMEM) for r in results))

    return jax.shard_map(
        body,
        mesh=mesh,
        in_specs=(
            P("slab", None),
            P("slab", None),
            P("view", None, None),
            P("view", None, None),
            P("view", "slab", None),
            P("view", "slab", None),
            P("slab", "view", None),
            P("slab", "view", None),
            P("slab", None),
            P("slab", None),
            P("slab", None),
            P("view", "slab", None),
        ),
        out_specs=(P("slab", None), P("slab", None)),
        check_vma=False,
    )


def solution(mesh):
    return build(mesh, 8, 4)
```
